256 devices in a mesh: seq: 32 (over z, y), head: 8 (over x, core).
Axes of the slice: x: 4, y: 4, z: 8, core: 2. Of those that a mesh axis runs over, the one named last changes fastest.
Arguments:
- queries: bfloat16 [32768, 3072], P('seq', 'head'), may hold values from -10 to 10
- keys: bfloat16 [32768, 3072], P('seq', 'head'), may hold values from -4 to 4
- values: bfloat16 [32768, 3072], P('seq', 'head'), may hold values from -4 to 4
- w_out: bfloat16 [3072, 3072], P('head', 'seq'), may hold values from -0.21875 to 0.21875
- head_kind: int32 [24], replicated, may hold values from 0 to 1, as said below
- band_offsets: int32 [2, 7], replicated, may hold values from -4 to 4, as said below
Outputs:
- mixed: bfloat16 [32768, 3072], P(('seq', 'head'))
The draws below stay inside these ranges and needn't reach their ends.
Inputs may be any that keep to these rules, and one draw needn't show every extreme that they name: `head_kind`: each group of 3 consecutive heads holds at most 2 temporal heads, and some group holds exactly that many. `band_offsets`: each row holds 7 distinct offsets and always contains 0, 4 and minus 4.
All inputs are finite; a program needn't handle non-finite values.
Results may differ from the reference program's by a relative error of at most 0.013.
Values may be sent and summed in bfloat16 or wider, within the bound.
A program may use at most 128 MiB of HBM per device.

```python
import math
import jax
import jax.numpy as jnp
from jax import lax

D = 3072
HEADS = 24
DH = 128
FRAMES = 16
BLK = 256
KOFF = 7
TOKENS = 32768
POSITIONS = 2048
RUN = 1024
QUOTA = 32
HEAD_DEV = 3
SPAN = 4
ATT = 3072
N_SEQ = 32
N_HEAD = 8


def draw_queries(key, part):
    noise = jax.random.normal(jax.random.fold_in(key, 11), (TOKENS, ATT)) * 2.5
    result = jnp.clip(noise, -10.0, 10.0)
    return result.astype(jnp.bfloat16)


def draw_keys(key, part):
    noise = jax.random.normal(jax.random.fold_in(key, 13), (TOKENS, ATT))
    result = jnp.clip(noise, -4.0, 4.0)
    return result.astype(jnp.bfloat16)


def draw_head_kind(key, part):
    groups = HEADS // HEAD_DEV
    counts = jax.random.randint(jax.random.fold_in(key, 21), (groups,), 0, HEAD_DEV)
    forced = jax.random.randint(jax.random.fold_in(key, 22), (), 0, groups)
    counts = jnp.where(jnp.arange(groups) == forced, HEAD_DEV - 1, counts)
    group_keys = jax.random.split(jax.random.fold_in(key, 23), groups)
    ranking = jax.vmap(lambda group_key: jax.random.permutation(group_key, HEAD_DEV))(group_keys)
    return (ranking < counts[:, None]).astype(jnp.int32).reshape(HEADS)


def draw_band_offsets(key, part):
    inner_steps = jnp.arange(1, SPAN, dtype=jnp.int32)
    candidates = jnp.concatenate([-inner_steps, inner_steps])
    fixed_part = jnp.array([0, -SPAN, SPAN], dtype=jnp.int32)
    offset_rows = []
    for head_type in range(2):
        picked = jax.random.permutation(jax.random.fold_in(key, 31 + head_type), candidates)[:KOFF - 3]
        offset_rows.append(jnp.concatenate([fixed_part, picked.astype(jnp.int32)]))
    return jnp.stack(offset_rows)


def block_levels(stream_key, extent, cuts, low, high):
    level, own = 1.0, jax.random.fold_in(stream_key, 6)
    for position, parts in cuts:
        draws = jnp.exp(jax.random.uniform(jax.random.fold_in(own, position), (parts,), jnp.float32, low / len(cuts), high / len(cuts)))
        level = level * jnp.repeat(draws, extent[position] // parts).reshape([-1 if axis == position else 1 for axis in range(len(extent))])
    return level


def scatter_about(stream_key, shape, deviation, most, pieces=(), held_as=jnp.bfloat16):
    level = block_levels(stream_key, shape, pieces, -0.22, 0.18) if pieces else 1.0
    values = jax.random.normal(stream_key, shape, jnp.float32) * deviation * level
    return jnp.minimum(jnp.maximum(values, -most), most).astype(held_as)


def setup_inputs(seed: int = 0) -> dict:
    arg_keys = jax.random.split(jax.random.key(seed), 7)
    return {
        "queries": draw_queries(jax.random.fold_in(arg_keys[6], 71), 0),
        "keys": draw_keys(jax.random.fold_in(arg_keys[6], 71), 0),
        "values": scatter_about(arg_keys[2], (TOKENS, ATT), 1.0, 4.0, ((0, 32), (1, 8))),
        "w_out": scatter_about(arg_keys[3], (ATT, D), (ATT // 4) ** -0.5, 0.21875, ((0, 8), (1, 32))),
        "head_kind": draw_head_kind(jax.random.fold_in(arg_keys[6], 71), 0),
        "band_offsets": draw_band_offsets(jax.random.fold_in(arg_keys[6], 71), 0),
    }


def to_temporal(field_rows):
    channels = field_rows.shape[1]
    grid_view = field_rows.reshape(FRAMES, POSITIONS // RUN, N_SEQ, QUOTA, channels)
    return grid_view.transpose(2, 1, 3, 0, 4).reshape(TOKENS, channels)

def from_temporal(field_rows):
    channels = field_rows.shape[1]
    grid_view = field_rows.reshape(N_SEQ, POSITIONS // RUN, QUOTA, FRAMES, channels)
    return grid_view.transpose(3, 1, 0, 2, 4).reshape(TOKENS, channels)

def band_attend(query_rows, key_rows, value_rows, offsets):
    block_count = TOKENS // BLK
    query_blocks = query_rows.reshape(block_count, BLK, DH)
    k_blocks = key_rows.reshape(block_count, BLK, DH)
    v_blocks = value_rows.reshape(block_count, BLK, DH)
    target = jnp.arange(block_count, dtype=jnp.int32)[:, None] + offsets[None, :]
    in_range = (target >= 0) & (target < block_count)
    key_index = jnp.clip(target, 0, block_count - 1).astype(jnp.int32)
    nearby_keys = jnp.take(k_blocks, key_index, axis=0).reshape(block_count, KOFF * BLK, DH)
    nearby_values = jnp.take(v_blocks, key_index, axis=0).reshape(block_count, KOFF * BLK, DH)
    score_scale = 1.0 / math.sqrt(DH)
    attention_scores = jnp.einsum('vuf,vzf->vuz', query_blocks.astype(jnp.float32), nearby_keys.astype(jnp.float32)) * score_scale
    allowed = jnp.broadcast_to(in_range[:, :, None], (block_count, KOFF, BLK)).reshape(block_count, 1, KOFF * BLK)
    attention_scores = jnp.where(allowed, attention_scores, -1e+30)
    row_max = lax.optimization_barrier(jnp.max(attention_scores, axis=2, keepdims=True))
    weights = jnp.exp(attention_scores - row_max)
    attention_probabilities = (weights / lax.optimization_barrier(jnp.sum(weights, axis=2, keepdims=True))).astype(jnp.bfloat16)
    attended_output = jnp.einsum('oyx,oxi->oyi', attention_probabilities.astype(jnp.float32), nearby_values.astype(jnp.float32))
    return attended_output.astype(jnp.bfloat16).reshape(TOKENS, DH)

def reference(queries, keys, values, w_out, head_kind, band_offsets):

    def one_head(head_items):
        query_rows, key_rows, value_rows, head_type = head_items
        temporal = head_type == 1
        offsets = jnp.where(temporal, band_offsets[1], band_offsets[0])
        query_rows = jnp.where(temporal, to_temporal(query_rows), query_rows)
        key_rows = jnp.where(temporal, to_temporal(key_rows), key_rows)
        value_rows = jnp.where(temporal, to_temporal(value_rows), value_rows)
        attended_output = band_attend(query_rows, key_rows, value_rows, offsets)
        return jnp.where(temporal, from_temporal(attended_output), attended_output)
    query_heads = queries.reshape(TOKENS, HEADS, DH).transpose(1, 0, 2)
    key_heads = keys.reshape(TOKENS, HEADS, DH).transpose(1, 0, 2)
    value_heads = values.reshape(TOKENS, HEADS, DH).transpose(1, 0, 2)
    per_head = lax.map(one_head, (query_heads, key_heads, value_heads, head_kind))
    attended_output = per_head.transpose(1, 0, 2).reshape(TOKENS, HEADS * DH)
    group_width = HEAD_DEV * DH

    def add_group(total, group):
        group_data = lax.dynamic_slice_in_dim(attended_output, group * group_width, group_width, 1)
        group_rows = lax.dynamic_slice_in_dim(w_out, group * group_width, group_width, 0)
        partial_value = jnp.dot(group_data, group_rows, preferred_element_type=jnp.float32).astype(jnp.bfloat16)
        partial_value = lax.optimization_barrier(partial_value)
        return (total + partial_value.astype(jnp.float32), None)
    total, unused = lax.scan(add_group, jnp.zeros((TOKENS, D), jnp.float32), jnp.arange(N_HEAD, dtype=jnp.int32))
    return total.astype(jnp.bfloat16)
```

```python
import math

import jax
import jax.numpy as jnp
from jax import lax
from jax.experimental import pallas as pl
from jax.experimental.pallas import tpu as pltpu
from jax.sharding import PartitionSpec as P

DH = 128
BLK = 256
NS = 32
KOFF = 7
BF = jnp.bfloat16
F32 = jnp.float32
MESH = pl.DeviceIdType.MESH
EXP_SCALE = math.log2(math.e) / math.sqrt(DH)


def pick(cond, yes, no):
    return jnp.where(cond, yes, no)


def kernel(kind_ref, offs_ref, q_ref, k_ref, v_ref, out_ref,
           snd, rcv, qx, kv0, kv1, kv2, att, ret,
           snd_sem, rcv_sem, halo_send, halo_recv, ret_send, ret_recv):
    s = lax.axis_index("seq")
    g = lax.axis_index("head")
    frame = s // 2
    half = s % 2
    kvs = (kv0, kv1, kv2)

    barrier = pltpu.get_barrier_semaphore()

    def greet(i, c):
        pl.semaphore_signal(barrier, inc=1, device_id={"seq": lax.rem(s + i, NS)}, device_id_type=MESH)
        return c

    lax.fori_loop(1, NS, greet, 0)

    kinds = [kind_ref[g * 3 + i] for i in range(3)]
    sp0 = kinds[0] == 0
    sp2 = jnp.logical_and(kinds[0] != 0, kinds[1] != 0)
    sp1 = jnp.logical_and(kinds[0] != 0, kinds[1] == 0)
    kind_slot = (jnp.where(sp0, kinds[1], kinds[0]), jnp.where(sp2, kinds[1], kinds[2]), 0)

    srcs = (q_ref, k_ref, v_ref)

    def prep(r, c):
        rows = pl.ds(pl.multiple_of(r * 128, 128), 128)
        for t in range(3):
            a = srcs[t][rows, 0:128]
            b = srcs[t][rows, 128:256]
            d = srcs[t][rows, 256:384]
            x0 = pick(sp0, b, a)
            x1 = pick(sp2, b, d)
            snd[0, pl.ds(r * 4, 4), t] = x0.reshape(4, 2, 16, DH)
            snd[1, pl.ds(r * 4, 4), t] = x1.reshape(4, 2, 16, DH)
            x2 = pick(sp0, a, pick(sp2, d, b)).reshape(8, 16, DH)
            blk = r // 2
            part = pl.ds((r % 2) * 8, 8)
            if t == 0:
                qx[2, blk, part] = x2
            else:
                kv2[t - 1, 4 + blk, part] = x2
        return c

    lax.fori_loop(0, 8, prep, 0)
    pl.semaphore_wait(barrier, NS - 1)

    def scatter(slot):
        def go(i, c):
            d = lax.rem(s + i, NS)
            pltpu.make_async_remote_copy(
                src_ref=snd.at[slot, d],
                dst_ref=rcv.at[slot, :, pl.ds(half * 2, 2), frame],
                send_sem=snd_sem.at[slot], recv_sem=rcv_sem.at[slot],
                device_id={"seq": d}, device_id_type=MESH).start()
            return c
        lax.fori_loop(1, NS, go, 0)
        pltpu.make_async_copy(
            snd.at[slot, s], rcv.at[slot, :, pl.ds(half * 2, 2), frame], rcv_sem.at[slot]).start()

    def halo(slot):
        kv = kvs[slot]
        ops = []
        for side in range(2):
            peer = lax.rem(s + (1 if side == 0 else NS - 1), NS)
            lo = 0 if side == 0 else 8
            op = pltpu.make_async_remote_copy(
                src_ref=kv.at[:, pl.ds(4, 4)],
                dst_ref=kv.at[:, pl.ds(lo, 4)],
                send_sem=halo_send.at[slot, side], recv_sem=halo_recv.at[slot, side],
                device_id={"seq": peer}, device_id_type=MESH)
            op.start()
            ops.append(op)
        return ops

    scatter(0)
    halo2 = halo(2)
    scatter(1)

    def attend(slot):
        kv = kvs[slot]
        offs = [jnp.where(kind_slot[slot] == 1, offs_ref[1, o], offs_ref[0, o]) for o in range(KOFF)]
        ones = jnp.ones((BLK, DH), BF)

        def block(j, c):
            q = qx[slot, j].reshape(BLK, DH)
            ks, vs, pens = [], [], []
            for o in range(KOFF):
                t = j + offs[o]
                gb = s * 4 + t
                ok = jnp.logical_and(gb >= 0, gb < NS * 4)
                idx = jnp.where(ok, t + 4, j + 4)
                ks.append(kv[0, idx].reshape(BLK, DH))
                vs.append(jnp.concatenate([kv[1, idx].reshape(BLK, DH), ones], axis=1))
                pens.append(jnp.where(ok, 0.0, 1e30).astype(F32))
            sc = [lax.dot_general(q, k, (((1,), (1,)), ((), ())), preferred_element_type=F32) for k in ks]
            m = sc[0]
            for x in sc[1:]:
                m = jnp.maximum(m, x)
            mx = jnp.max(m, axis=1, keepdims=True) * EXP_SCALE
            ps = [jnp.exp2(x * EXP_SCALE - (mx + pen)).astype(BF) for x, pen in zip(sc, pens)]
            acc = jnp.dot(jnp.concatenate(ps, axis=1), jnp.concatenate(vs, axis=0),
                          preferred_element_type=F32)
            o = (acc[:, :DH] / acc[:, DH:]).astype(BF)
            att[slot, j] = o.reshape(16, 16, DH)
            return c

        lax.fori_loop(0, 4, block, 0)

    def wait_halo(ops):
        for op in ops:
            op.wait()

    def arrive(slot):
        pltpu.make_async_copy(rcv.at[slot], rcv.at[slot], rcv_sem.at[slot]).wait()
        temporal = kind_slot[slot] == 1

        def sel(b, c):
            for t in range(3):
                local = snd[slot, pl.ds(b * 8, 8), t].reshape(16, 16, DH)
                x = pick(temporal, rcv[slot, t, b], local)
                if t == 0:
                    qx[slot, b] = x
                else:
                    kvs[slot][t - 1, 4 + b] = x
            return c

        lax.fori_loop(0, 4, sel, 0)

    def give_back(slot):
        def go(i, c):
            d = lax.rem(s + i, NS)
            pltpu.make_async_remote_copy(
                src_ref=att.at[slot, pl.ds((d % 2) * 2, 2), d // 2],
                dst_ref=ret.at[slot, s],
                send_sem=ret_send.at[slot], recv_sem=ret_recv.at[slot],
                device_id={"seq": d}, device_id_type=MESH).start()
            return c
        lax.fori_loop(1, NS, go, 0)
        pltpu.make_async_copy(
            att.at[slot, pl.ds(half * 2, 2), frame], ret.at[slot, s], ret_recv.at[slot]).start()

    wait_halo(halo2)
    attend(2)
    arrive(0)
    halo0 = halo(0)
    arrive(1)
    halo1 = halo(1)
    wait_halo(halo0)
    attend(0)
    give_back(0)
    wait_halo(halo1)
    attend(1)
    give_back(1)

    def finish2(b, c):
        out_ref[pl.ds(pl.multiple_of(b * BLK, BLK), BLK), 256:384] = att[2, b].reshape(BLK, DH)
        return c

    lax.fori_loop(0, 4, finish2, 0)

    for slot in range(2):
        pltpu.make_async_copy(ret.at[slot], ret.at[slot], ret_recv.at[slot]).wait()
        temporal = kind_slot[slot] == 1

        def fin(b, c):
            x = pick(temporal, ret[slot, pl.ds(b * 8, 8)].reshape(BLK, DH), att[slot, b].reshape(BLK, DH))
            out_ref[pl.ds(pl.multiple_of(b * BLK, BLK), BLK), slot * DH:(slot + 1) * DH] = x
            return c

        lax.fori_loop(0, 4, fin, 0)

    for slot in range(2):
        sent = snd.at[slot, pl.ds(0, NS - 1)]
        pltpu.make_async_copy(sent, sent, snd_sem.at[slot]).wait()
        back = ret.at[slot, pl.ds(0, NS - 1)]
        pltpu.make_async_copy(back, back, ret_send.at[slot]).wait()


def attention(queries, keys, values, head_kind, band_offsets):
    vm = pl.BlockSpec(memory_space=pltpu.VMEM)
    sm = pl.BlockSpec(memory_space=pltpu.SMEM)
    dma = pltpu.SemaphoreType.DMA
    return pl.pallas_call(
        kernel,
        out_shape=jax.ShapeDtypeStruct((1024, 384), BF),
        in_specs=[sm, sm, vm, vm, vm],
        out_specs=vm,
        scratch_shapes=[
            pltpu.VMEM((2, NS, 3, 2, 16, DH), BF),
            pltpu.VMEM((2, 3, 4, 16, 16, DH), BF),
            pltpu.VMEM((3, 4, 16, 16, DH), BF),
            pltpu.VMEM((2, 12, 16, 16, DH), BF),
            pltpu.VMEM((2, 12, 16, 16, DH), BF),
            pltpu.VMEM((2, 12, 16, 16, DH), BF),
            pltpu.VMEM((3, 4, 16, 16, DH), BF),
            pltpu.VMEM((2, NS, 2, 16, DH), BF),
            dma((2,)), dma((2,)), dma((3, 2)), dma((3, 2)), dma((2,)), dma((2,)),
        ],
        compiler_params=pltpu.CompilerParams(
            collective_id=0, has_side_effects=True, vmem_limit_bytes=60 * 1024 * 1024),
    )(head_kind, band_offsets, queries, keys, values)


def body(queries, keys, values, w_out, head_kind, band_offsets):
    head_rank = lax.axis_index("head")
    types = lax.dynamic_slice_in_dim(head_kind, head_rank * 3, 3)
    a, b, d = w_out[0:DH], w_out[DH:2 * DH], w_out[2 * DH:]
    sp0 = types[0] == 0
    sp2 = (types[0] != 0) & (types[1] != 0)
    rows = jnp.concatenate(
        [jnp.where(sp0, b, a), jnp.where(sp2, b, d), jnp.where(sp0, a, jnp.where(sp2, d, b))], axis=0)
    weight_rows = lax.all_gather(rows, "seq", axis=1, tiled=True)
    final_rows = attention(queries, keys, values, head_kind, band_offsets)
    return lax.psum_scatter(
        jnp.dot(final_rows, weight_rows, preferred_element_type=F32).astype(BF),
        "head", scatter_dimension=0, tiled=True)


def solution(mesh):
    return jax.shard_map(
        body,
        mesh=mesh,
        in_specs=(P("seq", "head"), P("seq", "head"), P("seq", "head"), P("head", "seq"), P(), P()),
        out_specs=P(("seq", "head"), None),
        check_vma=False,
    )
```

```python
import math

import jax
import jax.numpy as jnp
from jax import lax
from jax.experimental import pallas as pl
from jax.experimental.pallas import tpu as pltpu
from jax.sharding import PartitionSpec as P

DH = 128
BLK = 256
NS = 32
KOFF = 7
BF = jnp.bfloat16
F32 = jnp.float32
MESH = pl.DeviceIdType.MESH
EXP_SCALE = math.log2(math.e) / math.sqrt(DH)


def pick(cond, yes, no):
    return jnp.where(cond, yes, no)


def kernel(kind_ref, offs_ref, q_ref, k_ref, v_ref, w_ref, out_ref,
           snd, rcv, qx, kv0, kv1, kv2, att, ret, wbuf, fin, par, far_out, far_in, near_out, near_in, own,
           snd_sem, rcv_sem, halo_send, halo_recv, ret_send, ret_recv,
           wy_send, wy_recv, wr_send, wr_recv, wl_send, wl_recv, wp_send, wp_recv,
           ex_send, ex_recv, far_send, far_recv, near_send, near_recv):
    s = lax.axis_index("seq")
    g = lax.axis_index("head")
    frame = s // 2
    half = s % 2
    z = s // 4
    y = s % 4
    x = g // 2
    core = g % 2
    mate = {"head": x * 2 + 1 - core}
    x_up = {"head": lax.rem(x + 1, 4) * 2 + core}
    x_down = {"head": lax.rem(x + 3, 4) * 2 + core}
    kvs = (kv0, kv1, kv2)

    barrier = pltpu.get_barrier_semaphore()

    def greet(i, c):
        pl.semaphore_signal(barrier, inc=1, device_id={"seq": lax.rem(s + i, NS)}, device_id_type=MESH)
        return c

    lax.fori_loop(1, NS, greet, 0)
    for peer in (mate, x_up, x_down):
        pl.semaphore_signal(barrier, inc=1, device_id=peer, device_id_type=MESH)

    kinds = [kind_ref[g * 3 + i] for i in range(3)]
    sp0 = kinds[0] == 0
    sp2 = jnp.logical_and(kinds[0] != 0, kinds[1] != 0)
    sp1 = jnp.logical_and(kinds[0] != 0, kinds[1] == 0)
    kind_slot = (jnp.where(sp0, kinds[1], kinds[0]), jnp.where(sp2, kinds[1], kinds[2]), 0)

    srcs = (q_ref, k_ref, v_ref)

    def prep(r, c):
        rows = pl.ds(pl.multiple_of(r * 128, 128), 128)
        for t in range(3):
            a = srcs[t][rows, 0:128]
            b = srcs[t][rows, 128:256]
            d = srcs[t][rows, 256:384]
            x0 = pick(sp0, b, a)
            x1 = pick(sp2, b, d)
            snd[0, pl.ds(r * 4, 4), t] = x0.reshape(4, 2, 16, DH)
            snd[1, pl.ds(r * 4, 4), t] = x1.reshape(4, 2, 16, DH)
            x2 = pick(sp0, a, pick(sp2, d, b)).reshape(8, 16, DH)
            blk = r // 2
            part = pl.ds((r % 2) * 8, 8)
            if t == 0:
                qx[2, blk, part] = x2
            else:
                kv2[t - 1, 4 + blk, part] = x2
        return c

    lax.fori_loop(0, 8, prep, 0)
    wbuf[0, z, y] = w_ref[...]
    pl.semaphore_wait(barrier, NS + 2)

    def scatter(slot):
        def go(i, c):
            d = lax.rem(s + i, NS)
            pltpu.make_async_remote_copy(
                src_ref=snd.at[slot, d],
                dst_ref=rcv.at[slot, :, pl.ds(half * 2, 2), frame],
                send_sem=snd_sem.at[slot], recv_sem=rcv_sem.at[slot],
                device_id={"seq": d}, device_id_type=MESH).start()
            return c
        lax.fori_loop(1, NS, go, 0)
        pltpu.make_async_copy(
            snd.at[slot, s], rcv.at[slot, :, pl.ds(half * 2, 2), frame], rcv_sem.at[slot]).start()

    def halo(slot):
        kv = kvs[slot]
        ops = []
        for side in range(2):
            peer = lax.rem(s + (1 if side == 0 else NS - 1), NS)
            lo = 0 if side == 0 else 8
            op = pltpu.make_async_remote_copy(
                src_ref=kv.at[:, pl.ds(4, 4)],
                dst_ref=kv.at[:, pl.ds(lo, 4)],
                send_sem=halo_send.at[slot, side], recv_sem=halo_recv.at[slot, side],
                device_id={"seq": peer}, device_id_type=MESH)
            op.start()
            ops.append(op)
        return ops

    def attend(slot):
        kv = kvs[slot]
        offs = [jnp.where(kind_slot[slot] == 1, offs_ref[1, o], offs_ref[0, o]) for o in range(KOFF)]
        ones = jnp.ones((BLK, DH), BF)

        def block(j, c):
            q = qx[slot, j].reshape(BLK, DH)
            ks, vs, pens = [], [], []
            for o in range(KOFF):
                t = j + offs[o]
                gb = s * 4 + t
                ok = jnp.logical_and(gb >= 0, gb < NS * 4)
                idx = jnp.where(ok, t + 4, j + 4)
                ks.append(kv[0, idx].reshape(BLK, DH))
                vs.append(jnp.concatenate([kv[1, idx].reshape(BLK, DH), ones], axis=1))
                pens.append(jnp.where(ok, 0.0, 1e30).astype(F32))
            sc = [lax.dot_general(q, k, (((1,), (1,)), ((), ())), preferred_element_type=F32) for k in ks]
            m = sc[0]
            for x in sc[1:]:
                m = jnp.maximum(m, x)
            mx = jnp.max(m, axis=1, keepdims=True) * EXP_SCALE
            ps = [jnp.exp2(x * EXP_SCALE - (mx + pen)).astype(BF) for x, pen in zip(sc, pens)]
            acc = jnp.dot(jnp.concatenate(ps, axis=1), jnp.concatenate(vs, axis=0),
                          preferred_element_type=F32)
            o = (acc[:, :DH] / acc[:, DH:]).astype(BF)
            att[slot, j] = o.reshape(16, 16, DH)
            return c

        lax.fori_loop(0, 4, block, 0)

    def wait_halo(ops):
        for op in ops:
            op.wait()

    def arrive(slot):
        pltpu.make_async_copy(rcv.at[slot], rcv.at[slot], rcv_sem.at[slot]).wait()
        temporal = kind_slot[slot] == 1

        def sel(b, c):
            for t in range(3):
                local = snd[slot, pl.ds(b * 8, 8), t].reshape(16, 16, DH)
                x = pick(temporal, rcv[slot, t, b], local)
                if t == 0:
                    qx[slot, b] = x
                else:
                    kvs[slot][t - 1, 4 + b] = x
            return c

        lax.fori_loop(0, 4, sel, 0)

    def give_back(slot):
        def go(i, c):
            d = lax.rem(s + i, NS)
            pltpu.make_async_remote_copy(
                src_ref=att.at[slot, pl.ds((d % 2) * 2, 2), d // 2],
                dst_ref=ret.at[slot, s],
                send_sem=ret_send.at[slot], recv_sem=ret_recv.at[slot],
                device_id={"seq": d}, device_id_type=MESH).start()
            return c
        lax.fori_loop(1, NS, go, 0)
        pltpu.make_async_copy(
            att.at[slot, pl.ds(half * 2, 2), frame], ret.at[slot, s], ret_recv.at[slot]).start()

    def push(src_ref, dst_ref, send, recv, peer):
        op = pltpu.make_async_remote_copy(
            src_ref=src_ref, dst_ref=dst_ref, send_sem=send, recv_sem=recv,
            device_id=peer, device_id_type=MESH)
        op.start()
        return op

    y_up = {"seq": z * 4 + lax.rem(y + 1, 4)}
    y_down = {"seq": z * 4 + lax.rem(y + 3, 4)}
    z_up = {"seq": lax.rem(z + 1, 8) * 4 + y}
    z_down = {"seq": lax.rem(z + 7, 8) * 4 + y}

    def w_right(t):
        row = wbuf.at[0, lax.rem(z + 8 - t, 8)]
        return push(row, row, wr_send.at[t], wr_recv.at[t], z_up)

    def w_left(t):
        row = wbuf.at[0, lax.rem(z + t, 8)]
        return push(row, row, wl_send.at[t], wl_recv.at[t], z_down)

    def exchange(slot):
        return push(fin.at[slot, :, 1 - core], par.at[slot], ex_send.at[slot], ex_recv.at[slot], mate)

    def settle(slot):
        pltpu.make_async_copy(ret.at[slot], ret.at[slot], ret_recv.at[slot]).wait()
        temporal = kind_slot[slot] == 1

        def go(t, c):
            got = ret[slot, pl.ds(t * 4, 4)].reshape(DH, DH)
            mine = att[slot, t // 2, pl.ds((t % 2) * 8, 8)].reshape(DH, DH)
            fin[slot, t // 2, t % 2] = pick(temporal, got, mine)
            return c

        lax.fori_loop(0, 8, go, 0)

    wy0 = push(w_ref, wbuf.at[0, z, y], wy_send.at[0], wy_recv.at[0], y_up)
    wy1 = push(w_ref, wbuf.at[0, z, y], wy_send.at[1], wy_recv.at[1], y_down)
    scatter(0)
    halo2 = halo(2)
    scatter(1)
    wait_halo(halo2)
    attend(2)

    def spatial(t, c):
        fin[2, t // 2, t % 2] = att[2, t // 2, pl.ds((t % 2) * 8, 8)].reshape(DH, DH)
        return c

    lax.fori_loop(0, 8, spatial, 0)
    ex2 = exchange(2)
    arrive(0)
    halo0 = halo(0)
    wy0.wait_recv()
    piece = wbuf.at[0, z, lax.rem(y + 3, 4)]
    wy2 = push(piece, piece, wy_send.at[2], wy_recv.at[2], y_up)
    arrive(1)
    halo1 = halo(1)
    wy1.wait_recv()
    wy2.wait_recv()
    rights, lefts = [w_right(0)], [w_left(0)]
    wait_halo(halo0)
    attend(0)
    give_back(0)
    rights[0].wait_recv()
    lefts[0].wait_recv()
    rights.append(w_right(1))
    lefts.append(w_left(1))
    wait_halo(halo1)
    attend(1)
    give_back(1)
    rights[1].wait_recv()
    lefts[1].wait_recv()
    rights.append(w_right(2))
    lefts.append(w_left(2))
    settle(0)
    ex0 = exchange(0)
    rights[2].wait_recv()
    lefts[2].wait_recv()
    rights.append(w_right(3))
    settle(1)
    ex1 = exchange(1)
    rights[3].wait_recv()
    wp = push(wbuf.at[0], wbuf.at[1], wp_send, wp_recv, mate)
    for op in (ex2, ex0, ex1):
        op.wait_recv()
    wp.wait_recv()

    def part(dest, n):
        total = None
        for side in range(2):
            if side == 0:
                rows = [fin[i, dest, core] for i in range(3)]
            else:
                rows = [par[i, dest] for i in range(3)]
            wt = wbuf[side, pl.ds(2 * n, 2)].reshape(768, 384)
            p = lax.dot_general(jnp.concatenate(rows, axis=1), wt, (((1,), (1,)), ((), ())),
                                preferred_element_type=F32)
            total = p if total is None else total + p
        return total

    up, down, far = lax.rem(x + 1, 4), lax.rem(x + 3, 4), lax.rem(x + 2, 4)
    fars = []
    for n in (0, 2, 1, 3):
        far_out[n] = part(far, n).astype(BF)
        fars.append(push(far_out.at[n], far_in.at[n], far_send.at[n], far_recv.at[n], x_up if n < 2 else x_down))
    nears = []
    for n in range(2):
        near_out[0, 2 + n] = part(up, 2 + n).astype(BF)
        nears.append(push(near_out.at[0, 2 + n], near_in.at[0, 2 + n], near_send.at[0, 2 + n],
                          near_recv.at[0, 2 + n], x_up))
        near_out[1, n] = part(down, n).astype(BF)
        nears.append(push(near_out.at[1, n], near_in.at[1, n], near_send.at[1, n],
                          near_recv.at[1, n], x_down))
    for n in range(4):
        own[n] = part(x, n)
    for n in range(2):
        fars[0 if n == 0 else 2].wait_recv()
        near_out[0, n] = (part(up, n) + far_in[n].astype(F32)).astype(BF)
        nears.append(push(near_out.at[0, n], near_in.at[0, n], near_send.at[0, n],
                          near_recv.at[0, n], x_up))
        fars[1 if n == 0 else 3].wait_recv()
        near_out[1, 2 + n] = (part(down, 2 + n) + far_in[2 + n].astype(F32)).astype(BF)
        nears.append(push(near_out.at[1, 2 + n], near_in.at[1, 2 + n], near_send.at[1, 2 + n],
                          near_recv.at[1, 2 + n], x_down))
    for op in nears:
        op.wait_recv()
    for n in range(4):
        total = own[n] + near_in[0, n].astype(F32) + near_in[1, n].astype(F32)
        out_ref[:, n * 768:(n + 1) * 768] = total.astype(BF)

    for slot in range(2):
        sent = snd.at[slot, pl.ds(0, NS - 1)]
        pltpu.make_async_copy(sent, sent, snd_sem.at[slot]).wait()
        back = ret.at[slot, pl.ds(0, NS - 1)]
        pltpu.make_async_copy(back, back, ret_send.at[slot]).wait()
    for op in [wy0, wy1, wy2, wp, ex0, ex1, ex2] + rights + lefts + fars + nears:
        op.wait_send()


def attention(queries, keys, values, wt, head_kind, band_offsets):
    vm = pl.BlockSpec(memory_space=pltpu.VMEM)
    sm = pl.BlockSpec(memory_space=pltpu.SMEM)
    dma = pltpu.SemaphoreType.DMA
    return pl.pallas_call(
        kernel,
        out_shape=jax.ShapeDtypeStruct((128, 3072), BF),
        in_specs=[sm, sm, vm, vm, vm, vm],
        out_specs=vm,
        scratch_shapes=[
            pltpu.VMEM((2, NS, 3, 2, 16, DH), BF),
            pltpu.VMEM((2, 3, 4, 16, 16, DH), BF),
            pltpu.VMEM((3, 4, 16, 16, DH), BF),
            pltpu.VMEM((2, 12, 16, 16, DH), BF),
            pltpu.VMEM((2, 12, 16, 16, DH), BF),
            pltpu.VMEM((2, 12, 16, 16, DH), BF),
            pltpu.VMEM((3, 4, 16, 16, DH), BF),
            pltpu.VMEM((2, NS, 2, 16, DH), BF),
            pltpu.VMEM((2, 8, 4, 96, 384), BF),
            pltpu.VMEM((3, 4, 2, DH, DH), BF),
            pltpu.VMEM((3, 4, DH, DH), BF),
            pltpu.VMEM((4, DH, 768), BF),
            pltpu.VMEM((4, DH, 768), BF),
            pltpu.VMEM((2, 4, DH, 768), BF),
            pltpu.VMEM((2, 4, DH, 768), BF),
            pltpu.VMEM((4, DH, 768), F32),
            dma((2,)), dma((2,)), dma((3, 2)), dma((3, 2)), dma((2,)), dma((2,)),
            dma((3,)), dma((3,)), dma((4,)), dma((4,)), dma((3,)), dma((3,)), dma, dma,
            dma((3,)), dma((3,)), dma((4,)), dma((4,)), dma((2, 4)), dma((2, 4)),
        ],
        compiler_params=pltpu.CompilerParams(
            collective_id=0, has_side_effects=True, vmem_limit_bytes=60 * 1024 * 1024),
    )(head_kind, band_offsets, queries, keys, values, wt)


def body(queries, keys, values, w_out, head_kind, band_offsets):
    head_rank = lax.axis_index("head")
    types = lax.dynamic_slice_in_dim(head_kind, head_rank * 3, 3)
    a, b, d = w_out[0:DH], w_out[DH:2 * DH], w_out[2 * DH:]
    sp0 = types[0] == 0
    sp2 = (types[0] != 0) & (types[1] != 0)
    rows = jnp.concatenate(
        [jnp.where(sp0, b, a), jnp.where(sp2, b, d), jnp.where(sp0, a, jnp.where(sp2, d, b))], axis=0)
    return attention(queries, keys, values, rows.T, head_kind, band_offsets)


def solution(mesh):
    return jax.shard_map(
        body,
        mesh=mesh,
        in_specs=(P("seq", "head"), P("seq", "head"), P("seq", "head"), P("head", "seq"), P(), P()),
        out_specs=P(("seq", "head"), None),
        check_vma=False,
    )
```

```python
import math

import jax
import jax.numpy as jnp
from jax import lax
from jax.experimental import pallas as pl
from jax.experimental.pallas import tpu as pltpu
from jax.sharding import PartitionSpec as P

DH = 128
BLK = 256
NS = 32
KOFF = 7
BF = jnp.bfloat16
F32 = jnp.float32
MESH = pl.DeviceIdType.MESH
EXP_SCALE = math.log2(math.e) / math.sqrt(DH)


def pick(cond, yes, no):
    return jnp.where(cond, yes, no)


def kernel(kind_ref, offs_ref, q_ref, k_ref, v_ref, w_ref, out_ref,
           snd, rcv, qx, kv0, kv1, kv2, att, ret, wbuf, rly, fin, par, far_out, far_in, near_out, near_in, own,
           snd_sem, rcv_sem, halo_send, halo_recv, rly_send, rly_recv, fwd_send, ret_send, ret_recv,
           wy_send, wy_recv, wr_send, wr_recv, wl_send, wl_recv, wp_send, wp_recv,
           ex_send, ex_recv, far_send, far_recv, near_send, near_recv):
    s = lax.axis_index("seq")
    g = lax.axis_index("head")
    frame = s // 2
    half = s % 2
    z = s // 4
    y = s % 4
    x = g // 2
    core = g % 2
    mate = {"head": x * 2 + 1 - core}
    x_up = {"head": lax.rem(x + 1, 4) * 2 + core}
    x_down = {"head": lax.rem(x + 3, 4) * 2 + core}
    kvs = (kv0, kv1, kv2)

    barrier = pltpu.get_barrier_semaphore()

    def greet(i, c):
        pl.semaphore_signal(barrier, inc=1, device_id={"seq": lax.rem(s + i, NS)}, device_id_type=MESH)
        return c

    lax.fori_loop(1, NS, greet, 0)
    for peer in (mate, x_up, x_down):
        pl.semaphore_signal(barrier, inc=1, device_id=peer, device_id_type=MESH)

    kinds = [kind_ref[g * 3 + i] for i in range(3)]
    sp0 = kinds[0] == 0
    sp2 = jnp.logical_and(kinds[0] != 0, kinds[1] != 0)
    sp1 = jnp.logical_and(kinds[0] != 0, kinds[1] == 0)
    kind_slot = (jnp.where(sp0, kinds[1], kinds[0]), jnp.where(sp2, kinds[1], kinds[2]), 0)

    srcs = (q_ref, k_ref, v_ref)

    def prep(r, c):
        rows = pl.ds(pl.multiple_of(r * 128, 128), 128)
        for t in range(3):
            a = srcs[t][rows, 0:128]
            b = srcs[t][rows, 128:256]
            d = srcs[t][rows, 256:384]
            x0 = pick(sp0, b, a)
            x1 = pick(sp2, b, d)
            snd[0, pl.ds(r * 4, 4), t] = x0.reshape(4, 2, 16, DH)
            snd[1, pl.ds(r * 4, 4), t] = x1.reshape(4, 2, 16, DH)
            x2 = pick(sp0, a, pick(sp2, d, b)).reshape(8, 16, DH)
            blk = r // 2
            part = pl.ds((r % 2) * 8, 8)
            if t == 0:
                qx[2, blk, part] = x2
            else:
                kv2[t - 1, 4 + blk, part] = x2
        return c

    lax.fori_loop(0, 8, prep, 0)
    wa, wb, wd = w_ref[0:DH], w_ref[DH:2 * DH], w_ref[2 * DH:]
    w_rows = jnp.concatenate(
        [pick(sp0, wb, wa), pick(sp2, wb, wd), pick(sp0, wa, pick(sp2, wd, wb))], axis=0)
    eye = (lax.broadcasted_iota(jnp.int32, (96, 96), 0)
           == lax.broadcasted_iota(jnp.int32, (96, 96), 1)).astype(F32).astype(BF)
    wbuf[0, z, y] = lax.dot_general(
        eye, w_rows, (((1,), (1,)), ((), ())), preferred_element_type=F32).astype(BF)
    pl.semaphore_wait(barrier, NS + 2)

    def scatter(slot):
        def go(i, c):
            d = lax.rem(s + i, NS)
            pltpu.make_async_remote_copy(
                src_ref=snd.at[slot, d],
                dst_ref=rcv.at[slot, :, pl.ds(half * 2, 2), frame],
                send_sem=snd_sem.at[slot], recv_sem=rcv_sem.at[slot],
                device_id={"seq": d}, device_id_type=MESH).start()
            return c
        lax.fori_loop(1, NS, go, 0)
        pltpu.make_async_copy(
            snd.at[slot, s], rcv.at[slot, :, pl.ds(half * 2, 2), frame], rcv_sem.at[slot]).start()

    edge = (y == 3, y == 0)
    hop = (1, NS - 1)
    lows = (0, 8)

    def halo(slot):
        kv = kvs[slot]
        for side in range(2):
            lo = lows[side]
            peer = lax.rem(s + hop[side], NS)
            pltpu.make_async_remote_copy(
                src_ref=kv.at[:, pl.ds(4, 2)], dst_ref=kv.at[:, pl.ds(lo, 2)],
                send_sem=halo_send.at[slot, side], recv_sem=halo_recv.at[slot, side],
                device_id={"seq": peer}, device_id_type=MESH).start()

            @pl.when(jnp.logical_not(edge[side]))
            def _():
                pltpu.make_async_remote_copy(
                    src_ref=kv.at[:, pl.ds(6, 2)], dst_ref=kv.at[:, pl.ds(lo + 2, 2)],
                    send_sem=halo_send.at[slot, side], recv_sem=halo_recv.at[slot, side],
                    device_id={"seq": peer}, device_id_type=MESH).start()

            @pl.when(edge[side])
            def _():
                pltpu.make_async_remote_copy(
                    src_ref=kv.at[:, pl.ds(6, 2)], dst_ref=rly.at[slot],
                    send_sem=halo_send.at[slot, side], recv_sem=rly_recv.at[slot],
                    device_id={"seq": z * 4 + (0 if side == 0 else 3)}, device_id_type=MESH).start()

    def relay(slot):
        kv = kvs[slot]
        for side in range(2):
            lo = lows[side]

            @pl.when(edge[1 - side])
            def _():
                pltpu.make_async_copy(rly.at[slot], rly.at[slot], rly_recv.at[slot]).wait()
                pltpu.make_async_remote_copy(
                    src_ref=rly.at[slot], dst_ref=kv.at[:, pl.ds(lo + 2, 2)],
                    send_sem=fwd_send.at[slot], recv_sem=halo_recv.at[slot, side],
                    device_id={"seq": lax.rem(z + (1 if side == 0 else 7), 8) * 4 + y},
                    device_id_type=MESH).start()

    def wait_halo(slot):
        kv = kvs[slot]
        for side in range(2):
            got = kv.at[:, pl.ds(lows[side], 4)]
            pltpu.make_async_copy(got, got, halo_recv.at[slot, side]).wait()

    def attend(slot):
        kv = kvs[slot]
        offs = [jnp.where(kind_slot[slot] == 1, offs_ref[1, o], offs_ref[0, o]) for o in range(KOFF)]
        ones = jnp.ones((BLK, DH), BF)

        def block(j, c):
            q = qx[slot, j].reshape(BLK, DH)
            ks, vs, pens = [], [], []
            for o in range(KOFF):
                t = j + offs[o]
                gb = s * 4 + t
                ok = jnp.logical_and(gb >= 0, gb < NS * 4)
                idx = jnp.where(ok, t + 4, j + 4)
                ks.append(kv[0, idx].reshape(BLK, DH))
                vs.append(jnp.concatenate([kv[1, idx].reshape(BLK, DH), ones], axis=1))
                pens.append(jnp.where(ok, 0.0, 1e30).astype(F32))
            sc = [lax.dot_general(q, k, (((1,), (1,)), ((), ())), preferred_element_type=F32) for k in ks]
            m = sc[0]
            for x in sc[1:]:
                m = jnp.maximum(m, x)
            mx = jnp.max(m, axis=1, keepdims=True) * EXP_SCALE
            ps = [jnp.exp2(x * EXP_SCALE - (mx + pen)).astype(BF) for x, pen in zip(sc, pens)]
            acc = jnp.dot(jnp.concatenate(ps, axis=1), jnp.concatenate(vs, axis=0),
                          preferred_element_type=F32)
            o = (acc[:, :DH] / acc[:, DH:]).astype(BF)
            att[slot, j] = o.reshape(16, 16, DH)
            return c

        lax.fori_loop(0, 4, block, 0)

    def wait_slot(slot):
        pltpu.make_async_copy(rcv.at[slot], rcv.at[slot], rcv_sem.at[slot]).wait()

    def choose(slot):
        temporal = kind_slot[slot] == 1

        def sel(b, c):
            for t in range(3):
                local = snd[slot, pl.ds(b * 8, 8), t].reshape(16, 16, DH)
                x = pick(temporal, rcv[slot, t, b], local)
                if t == 0:
                    qx[slot, b] = x
                else:
                    kvs[slot][t - 1, 4 + b] = x
            return c

        lax.fori_loop(0, 4, sel, 0)

    def give_back(slot):
        def go(i, c):
            d = lax.rem(s + i, NS)
            pltpu.make_async_remote_copy(
                src_ref=att.at[slot, pl.ds((d % 2) * 2, 2), d // 2],
                dst_ref=ret.at[slot, s],
                send_sem=ret_send.at[slot], recv_sem=ret_recv.at[slot],
                device_id={"seq": d}, device_id_type=MESH).start()
            return c
        lax.fori_loop(1, NS, go, 0)
        pltpu.make_async_copy(
            att.at[slot, pl.ds(half * 2, 2), frame], ret.at[slot, s], ret_recv.at[slot]).start()

    def push(src_ref, dst_ref, send, recv, peer):
        op = pltpu.make_async_remote_copy(
            src_ref=src_ref, dst_ref=dst_ref, send_sem=send, recv_sem=recv,
            device_id=peer, device_id_type=MESH)
        op.start()
        return op

    y_up = {"seq": z * 4 + lax.rem(y + 1, 4)}
    y_down = {"seq": z * 4 + lax.rem(y + 3, 4)}
    z_up = {"seq": lax.rem(z + 1, 8) * 4 + y}
    z_down = {"seq": lax.rem(z + 7, 8) * 4 + y}

    def w_right(t):
        row = wbuf.at[0, lax.rem(z + 8 - t, 8)]
        return push(row, row, wr_send.at[t], wr_recv.at[t], z_up)

    def w_left(t):
        row = wbuf.at[0, lax.rem(z + t, 8)]
        return push(row, row, wl_send.at[t], wl_recv.at[t], z_down)

    def exchange(slot):
        return push(fin.at[slot, :, 1 - core], par.at[slot], ex_send.at[slot], ex_recv.at[slot], mate)

    def settle(slot):
        pltpu.make_async_copy(ret.at[slot], ret.at[slot], ret_recv.at[slot]).wait()
        temporal = kind_slot[slot] == 1

        def go(t, c):
            got = ret[slot, pl.ds(t * 4, 4)].reshape(DH, DH)
            mine = att[slot, t // 2, pl.ds((t % 2) * 8, 8)].reshape(DH, DH)
            fin[slot, t // 2, t % 2] = pick(temporal, got, mine)
            return c

        lax.fori_loop(0, 8, go, 0)

    passed = []

    def pass_row(r):
        passed.append(push(wbuf.at[0, r], wbuf.at[1, r], wp_send.at[len(passed)], wp_recv.at[r], mate))

    def z_step(t):
        if t > 0:
            rights[t - 1].wait_recv()
            if t <= 3:
                lefts[t - 1].wait_recv()
        if t < 4:
            rights.append(w_right(t))
        if t < 3:
            lefts.append(w_left(t))
        if t > 0:
            pass_row(lax.rem(z + 8 - t, 8))
            if t <= 3:
                pass_row(lax.rem(z + t, 8))
        else:
            pass_row(z)

    rights, lefts = [], []
    mine = wbuf.at[0, z, y]
    scatter(0)
    halo(2)
    wy0 = push(mine, mine, wy_send.at[0], wy_recv.at[0], y_up)
    wy1 = push(mine, mine, wy_send.at[1], wy_recv.at[1], y_down)
    relay(2)
    wait_slot(0)
    scatter(1)
    choose(0)
    halo(0)
    wy0.wait_recv()
    piece = wbuf.at[0, z, lax.rem(y + 3, 4)]
    wy2 = push(piece, piece, wy_send.at[2], wy_recv.at[2], y_up)
    wait_halo(2)
    attend(2)

    def spatial(t, c):
        fin[2, t // 2, t % 2] = att[2, t // 2, pl.ds((t % 2) * 8, 8)].reshape(DH, DH)
        return c

    lax.fori_loop(0, 8, spatial, 0)
    ex2 = exchange(2)
    relay(0)
    wait_slot(1)
    choose(1)
    halo(1)
    wy1.wait_recv()
    wy2.wait_recv()
    z_step(0)
    wait_halo(0)
    attend(0)
    relay(1)
    z_step(1)
    wait_halo(1)
    give_back(0)
    attend(1)
    give_back(1)
    z_step(2)
    settle(0)
    ex0 = exchange(0)
    z_step(3)
    settle(1)
    ex1 = exchange(1)
    z_step(4)
    for op in (ex2, ex0, ex1):
        op.wait_recv()
    for r in range(8):
        row = wbuf.at[1, r]
        pltpu.make_async_copy(row, row, wp_recv.at[r]).wait()

    def part(dest, n):
        total = None
        for side in range(2):
            if side == 0:
                rows = [fin[i, dest, core] for i in range(3)]
            else:
                rows = [par[i, dest] for i in range(3)]
            wt = wbuf[side, pl.ds(2 * n, 2)].reshape(768, 384)
            p = lax.dot_general(jnp.concatenate(rows, axis=1), wt, (((1,), (1,)), ((), ())),
                                preferred_element_type=F32)
            total = p if total is None else total + p
        return total

    up, down, far = lax.rem(x + 1, 4), lax.rem(x + 3, 4), lax.rem(x + 2, 4)
    fars = []
    for n in (0, 2, 1, 3):
        far_out[n] = part(far, n).astype(BF)
        fars.append(push(far_out.at[n], far_in.at[n], far_send.at[n], far_recv.at[n], x_up if n < 2 else x_down))
    nears = []
    for n in range(2):
        near_out[0, 2 + n] = part(up, 2 + n).astype(BF)
        nears.append(push(near_out.at[0, 2 + n], near_in.at[0, 2 + n], near_send.at[0, 2 + n],
                          near_recv.at[0, 2 + n], x_up))
        near_out[1, n] = part(down, n).astype(BF)
        nears.append(push(near_out.at[1, n], near_in.at[1, n], near_send.at[1, n],
                          near_recv.at[1, n], x_down))
    for n in range(4):
        own[n] = part(x, n)
    for n in range(2):
        fars[0 if n == 0 else 2].wait_recv()
        near_out[0, n] = (part(up, n) + far_in[n].astype(F32)).astype(BF)
        nears.append(push(near_out.at[0, n], near_in.at[0, n], near_send.at[0, n],
                          near_recv.at[0, n], x_up))
        fars[1 if n == 0 else 3].wait_recv()
        near_out[1, 2 + n] = (part(down, 2 + n) + far_in[2 + n].astype(F32)).astype(BF)
        nears.append(push(near_out.at[1, 2 + n], near_in.at[1, 2 + n], near_send.at[1, 2 + n],
                          near_recv.at[1, 2 + n], x_down))
    for op in nears:
        op.wait_recv()
    for n in range(4):
        total = own[n] + near_in[0, n].astype(F32) + near_in[1, n].astype(F32)
        out_ref[:, n * 768:(n + 1) * 768] = total.astype(BF)

    for slot in range(2):
        sent = snd.at[slot, pl.ds(0, NS - 1)]
        pltpu.make_async_copy(sent, sent, snd_sem.at[slot]).wait()
        back = ret.at[slot, pl.ds(0, NS - 1)]
        pltpu.make_async_copy(back, back, ret_send.at[slot]).wait()
    for slot in range(3):
        kv = kvs[slot]
        for side in range(2):
            out = kv.at[:, pl.ds(4, 4)]
            pltpu.make_async_copy(out, out, halo_send.at[slot, side]).wait()

            @pl.when(edge[1 - side])
            def _():
                pltpu.make_async_copy(rly.at[slot], rly.at[slot], fwd_send.at[slot]).wait()
    for op in [wy0, wy1, wy2, ex0, ex1, ex2] + passed + rights + lefts + fars + nears:
        op.wait_send()


def attention(queries, keys, values, wt, head_kind, band_offsets):
    vm = pl.BlockSpec(memory_space=pltpu.VMEM)
    sm = pl.BlockSpec(memory_space=pltpu.SMEM)
    dma = pltpu.SemaphoreType.DMA
    return pl.pallas_call(
        kernel,
        out_shape=jax.ShapeDtypeStruct((128, 3072), BF),
        in_specs=[sm, sm, vm, vm, vm, vm],
        out_specs=vm,
        scratch_shapes=[
            pltpu.VMEM((2, NS, 3, 2, 16, DH), BF),
            pltpu.VMEM((2, 3, 4, 16, 16, DH), BF),
            pltpu.VMEM((3, 4, 16, 16, DH), BF),
            pltpu.VMEM((2, 12, 16, 16, DH), BF),
            pltpu.VMEM((2, 12, 16, 16, DH), BF),
            pltpu.VMEM((2, 12, 16, 16, DH), BF),
            pltpu.VMEM((3, 4, 16, 16, DH), BF),
            pltpu.VMEM((2, NS, 2, 16, DH), BF),
            pltpu.VMEM((2, 8, 4, 96, 384), BF),
            pltpu.VMEM((3, 2, 2, 16, 16, DH), BF),
            pltpu.VMEM((3, 4, 2, DH, DH), BF),
            pltpu.VMEM((3, 4, DH, DH), BF),
            pltpu.VMEM((4, DH, 768), BF),
            pltpu.VMEM((4, DH, 768), BF),
            pltpu.VMEM((2, 4, DH, 768), BF),
            pltpu.VMEM((2, 4, DH, 768), BF),
            pltpu.VMEM((4, DH, 768), F32),
            dma((2,)), dma((2,)), dma((3, 2)), dma((3, 2)), dma((3,)), dma((3,)), dma((3,)),
            dma((2,)), dma((2,)),
            dma((3,)), dma((3,)), dma((4,)), dma((4,)), dma((3,)), dma((3,)), dma((8,)), dma((8,)),
            dma((3,)), dma((3,)), dma((4,)), dma((4,)), dma((2, 4)), dma((2, 4)),
        ],
        compiler_params=pltpu.CompilerParams(
            collective_id=0, has_side_effects=True, vmem_limit_bytes=60 * 1024 * 1024),
    )(head_kind, band_offsets, queries, keys, values, wt)


def body(queries, keys, values, w_out, head_kind, band_offsets):
    return attention(queries, keys, values, w_out, head_kind, band_offsets)


def solution(mesh):
    return jax.shard_map(
        body,
        mesh=mesh,
        in_specs=(P("seq", "head"), P("seq", "head"), P("seq", "head"), P("head", "seq"), P(), P()),
        out_specs=P(("seq", "head"), None),
        check_vma=False,
    )
```

```python
import math

import jax
import jax.numpy as jnp
from jax import lax
from jax.experimental import pallas as pl
from jax.experimental.pallas import tpu as pltpu
from jax.sharding import PartitionSpec as P

DH = 128
BLK = 256
NS = 32
KOFF = 7
BF = jnp.bfloat16
F32 = jnp.float32
MESH = pl.DeviceIdType.MESH
EXP_SCALE = math.log2(math.e) / math.sqrt(DH)


def pick(cond, yes, no):
    return jnp.where(cond, yes, no)


def kernel(kind_ref, offs_ref, q_ref, k_ref, v_ref, w_ref, out_ref,
           snd, rcv, qx, kv0, kv1, kv2, att, ret, wbuf, rly, fin, par, far_out, far_in, near_out, near_in, own,
           snd_sem, rcv_sem, halo_send, halo_recv, rly_send, rly_recv, fwd_send, ret_send, ret_recv,
           wy_send, wy_recv, wr_send, wr_recv, wl_send, wl_recv, wp_send, wp_recv,
           ex_send, ex_recv, far_send, far_recv, near_send, near_recv):
    s = lax.axis_index("seq")
    g = lax.axis_index("head")
    frame = s // 2
    half = s % 2
    z = s // 4
    y = s % 4
    x = g // 2
    core = g % 2
    mate = {"head": x * 2 + 1 - core}
    x_up = {"head": lax.rem(x + 1, 4) * 2 + core}
    x_down = {"head": lax.rem(x + 3, 4) * 2 + core}
    kvs = (kv0, kv1, kv2)

    barrier = pltpu.get_barrier_semaphore()

    def greet(i, c):
        pl.semaphore_signal(barrier, inc=1, device_id={"seq": lax.rem(s + i, NS)}, device_id_type=MESH)
        return c

    lax.fori_loop(1, NS, greet, 0)
    for peer in (mate, x_up, x_down):
        pl.semaphore_signal(barrier, inc=1, device_id=peer, device_id_type=MESH)

    kinds = [kind_ref[g * 3 + i] for i in range(3)]
    sp0 = kinds[0] == 0
    sp2 = jnp.logical_and(kinds[0] != 0, kinds[1] != 0)
    sp1 = jnp.logical_and(kinds[0] != 0, kinds[1] == 0)
    kind_slot = (jnp.where(sp0, kinds[1], kinds[0]), jnp.where(sp2, kinds[1], kinds[2]), 0)

    srcs = (q_ref, k_ref, v_ref)

    def prep(r, c):
        rows = pl.ds(pl.multiple_of(r * 128, 128), 128)
        for t in range(3):
            a = srcs[t][rows, 0:128]
            b = srcs[t][rows, 128:256]
            d = srcs[t][rows, 256:384]
            x0 = pick(sp0, b, a)
            x1 = pick(sp2, b, d)
            snd[0, pl.ds(r * 4, 4), t] = x0.reshape(4, 2, 16, DH)
            snd[1, pl.ds(r * 4, 4), t] = x1.reshape(4, 2, 16, DH)
            x2 = pick(sp0, a, pick(sp2, d, b)).reshape(8, 16, DH)
            blk = r // 2
            part = pl.ds((r % 2) * 8, 8)
            if t == 0:
                qx[2, blk, part] = x2
            else:
                kv2[t - 1, 4 + blk, part] = x2
        return c

    lax.fori_loop(0, 8, prep, 0)
    wa, wb, wd = w_ref[0:DH], w_ref[DH:2 * DH], w_ref[2 * DH:]
    w_rows = jnp.concatenate(
        [pick(sp0, wb, wa), pick(sp2, wb, wd), pick(sp0, wa, pick(sp2, wd, wb))], axis=0)
    eye = (lax.broadcasted_iota(jnp.int32, (96, 96), 0)
           == lax.broadcasted_iota(jnp.int32, (96, 96), 1)).astype(F32).astype(BF)
    wbuf[0, z, y] = lax.dot_general(
        eye, w_rows, (((1,), (1,)), ((), ())), preferred_element_type=F32).astype(BF)
    pl.semaphore_wait(barrier, NS + 2)

    def scatter(slot):
        def go(i, c):
            d = lax.rem(s + i, NS)
            pltpu.make_async_remote_copy(
                src_ref=snd.at[slot, d],
                dst_ref=rcv.at[slot, :, pl.ds(half * 2, 2), frame],
                send_sem=snd_sem.at[slot], recv_sem=rcv_sem.at[slot],
                device_id={"seq": d}, device_id_type=MESH).start()
            return c
        lax.fori_loop(1, NS, go, 0)
        pltpu.make_async_copy(
            snd.at[slot, s], rcv.at[slot, :, pl.ds(half * 2, 2), frame], rcv_sem.at[slot]).start()

    edge = (y == 3, y == 0)
    hop = (1, NS - 1)
    lows = (0, 8)

    def halo(slot):
        kv = kvs[slot]
        for side in range(2):
            lo = lows[side]
            peer = lax.rem(s + hop[side], NS)
            pltpu.make_async_remote_copy(
                src_ref=kv.at[:, pl.ds(4, 2)], dst_ref=kv.at[:, pl.ds(lo, 2)],
                send_sem=halo_send.at[slot, side], recv_sem=halo_recv.at[slot, side],
                device_id={"seq": peer}, device_id_type=MESH).start()

            @pl.when(jnp.logical_not(edge[side]))
            def _():
                pltpu.make_async_remote_copy(
                    src_ref=kv.at[:, pl.ds(6, 2)], dst_ref=kv.at[:, pl.ds(lo + 2, 2)],
                    send_sem=halo_send.at[slot, side], recv_sem=halo_recv.at[slot, side],
                    device_id={"seq": peer}, device_id_type=MESH).start()

            @pl.when(edge[side])
            def _():
                pltpu.make_async_remote_copy(
                    src_ref=kv.at[:, pl.ds(6, 2)], dst_ref=rly.at[slot],
                    send_sem=halo_send.at[slot, side], recv_sem=rly_recv.at[slot],
                    device_id={"seq": z * 4 + (0 if side == 0 else 3)}, device_id_type=MESH).start()

    def relay(slot):
        kv = kvs[slot]
        for side in range(2):
            lo = lows[side]

            @pl.when(edge[1 - side])
            def _():
                pltpu.make_async_copy(rly.at[slot], rly.at[slot], rly_recv.at[slot]).wait()
                pltpu.make_async_remote_copy(
                    src_ref=rly.at[slot], dst_ref=kv.at[:, pl.ds(lo + 2, 2)],
                    send_sem=fwd_send.at[slot], recv_sem=halo_recv.at[slot, side],
                    device_id={"seq": lax.rem(z + (1 if side == 0 else 7), 8) * 4 + y},
                    device_id_type=MESH).start()

    def wait_halo(slot):
        kv = kvs[slot]
        for side in range(2):
            got = kv.at[:, pl.ds(lows[side], 4)]
            pltpu.make_async_copy(got, got, halo_recv.at[slot, side]).wait()

    def attend(slot, first=0, last=4):
        kv = kvs[slot]
        offs = [jnp.where(kind_slot[slot] == 1, offs_ref[1, o], offs_ref[0, o]) for o in range(KOFF)]
        ones = jnp.ones((BLK, DH), BF)

        def block(j, c):
            q = qx[slot, j].reshape(BLK, DH)
            ks, vs, pens = [], [], []
            for o in range(KOFF):
                t = j + offs[o]
                gb = s * 4 + t
                ok = jnp.logical_and(gb >= 0, gb < NS * 4)
                idx = jnp.where(ok, t + 4, j + 4)
                ks.append(kv[0, idx].reshape(BLK, DH))
                vs.append(jnp.concatenate([kv[1, idx].reshape(BLK, DH), ones], axis=1))
                pens.append(jnp.where(ok, 0.0, 1e30).astype(F32))
            sc = [lax.dot_general(q, k, (((1,), (1,)), ((), ())), preferred_element_type=F32) for k in ks]
            m = sc[0]
            for x in sc[1:]:
                m = jnp.maximum(m, x)
            mx = jnp.max(m, axis=1, keepdims=True) * EXP_SCALE
            ps = [jnp.exp2(x * EXP_SCALE - (mx + pen)).astype(BF) for x, pen in zip(sc, pens)]
            acc = jnp.dot(jnp.concatenate(ps, axis=1), jnp.concatenate(vs, axis=0),
                          preferred_element_type=F32)
            o = (acc[:, :DH] / acc[:, DH:]).astype(BF)
            att[slot, j] = o.reshape(16, 16, DH)
            return c

        lax.fori_loop(first, last, block, 0)

    def wait_slot(slot):
        pltpu.make_async_copy(rcv.at[slot], rcv.at[slot], rcv_sem.at[slot]).wait()

    def choose(slot):
        temporal = kind_slot[slot] == 1

        def sel(b, c):
            for t in range(3):
                local = snd[slot, pl.ds(b * 8, 8), t].reshape(16, 16, DH)
                x = pick(temporal, rcv[slot, t, b], local)
                if t == 0:
                    qx[slot, b] = x
                else:
                    kvs[slot][t - 1, 4 + b] = x
            return c

        lax.fori_loop(0, 4, sel, 0)

    def give_back(slot, side):
        def go(i, c):
            to = lax.rem(frame + i, 16)
            pltpu.make_async_remote_copy(
                src_ref=att.at[slot, side * 2:side * 2 + 2, to],
                dst_ref=ret.at[slot, s],
                send_sem=ret_send.at[slot], recv_sem=ret_recv.at[slot],
                device_id={"seq": to * 2 + side}, device_id_type=MESH).start()
            return c
        lax.fori_loop(1, 16, go, 0)

        @pl.when(half == side)
        def _():
            pltpu.make_async_copy(
                att.at[slot, side * 2:side * 2 + 2, frame], ret.at[slot, s], ret_recv.at[slot]).start()

        @pl.when(half != side)
        def _():
            pltpu.make_async_remote_copy(
                src_ref=att.at[slot, side * 2:side * 2 + 2, frame],
                dst_ref=ret.at[slot, s],
                send_sem=ret_send.at[slot], recv_sem=ret_recv.at[slot],
                device_id={"seq": frame * 2 + side}, device_id_type=MESH).start()

    def push(src_ref, dst_ref, send, recv, peer):
        op = pltpu.make_async_remote_copy(
            src_ref=src_ref, dst_ref=dst_ref, send_sem=send, recv_sem=recv,
            device_id=peer, device_id_type=MESH)
        op.start()
        return op

    y_up = {"seq": z * 4 + lax.rem(y + 1, 4)}
    y_down = {"seq": z * 4 + lax.rem(y + 3, 4)}
    z_up = {"seq": lax.rem(z + 1, 8) * 4 + y}
    z_down = {"seq": lax.rem(z + 7, 8) * 4 + y}

    def w_right(t):
        row = wbuf.at[0, lax.rem(z + 8 - t, 8), y]
        return push(row, row, wr_send.at[t], wr_recv.at[t], z_up)

    def w_left(t):
        row = wbuf.at[0, lax.rem(z + t, 8), y]
        return push(row, row, wl_send.at[t], wl_recv.at[t], z_down)

    def exchange(slot):
        return push(fin.at[slot, :, 1 - core], par.at[slot], ex_send.at[slot], ex_recv.at[slot], mate)

    def settle(slot):
        pltpu.make_async_copy(ret.at[slot], ret.at[slot], ret_recv.at[slot]).wait()
        temporal = kind_slot[slot] == 1

        def go(t, c):
            got = ret[slot, pl.ds(t * 4, 4)].reshape(DH, DH)
            mine = att[slot, t // 2, pl.ds((t % 2) * 8, 8)].reshape(DH, DH)
            fin[slot, t // 2, t % 2] = pick(temporal, got, mine)
            return c

        lax.fori_loop(0, 8, go, 0)

    passed = []
    columns = (y, lax.rem(y + 3, 4), lax.rem(y + 1, 4), lax.rem(y + 2, 4))

    def pass_column(i):
        passed.append(push(wbuf.at[0, :, columns[i]], wbuf.at[1, :, columns[i]],
                           wp_send.at[i], wp_recv.at[i], mate))

    def z_step(t):
        if t > 0:
            rights[t - 1].wait_recv()
            if t <= 3:
                lefts[t - 1].wait_recv()
        if t < 4:
            rights.append(w_right(t))
        if t < 3:
            lefts.append(w_left(t))

    def y_step(t):
        if t == 0:
            part = wbuf.at[0, :, y]
            ys.append(push(part, part, wy_send.at[0], wy_recv.at[0], y_up))
            ys.append(push(part, part, wy_send.at[1], wy_recv.at[1], y_down))
            pass_column(0)
        elif t == 1:
            ys[0].wait_recv()
            part = wbuf.at[0, pl.ds(0, 4), columns[1]]
            ys.append(push(part, part, wy_send.at[2], wy_recv.at[2], y_up))
            ys[1].wait_recv()
            part = wbuf.at[0, pl.ds(4, 4), columns[2]]
            ys.append(push(part, part, wy_send.at[3], wy_recv.at[3], y_down))
            pass_column(1)
            pass_column(2)
        else:
            ys[2].wait_recv()
            ys[3].wait_recv()
            pass_column(3)

    rights, lefts, ys = [], [], []
    scatter(0)
    z_step(0)
    halo(2)
    relay(2)
    wait_slot(0)
    scatter(1)
    choose(0)
    halo(0)
    z_step(1)
    wait_halo(2)
    attend(2)

    def spatial(t, c):
        fin[2, t // 2, t % 2] = att[2, t // 2, pl.ds((t % 2) * 8, 8)].reshape(DH, DH)
        return c

    lax.fori_loop(0, 8, spatial, 0)
    ex2 = exchange(2)
    z_step(2)
    relay(0)
    wait_slot(1)
    choose(1)
    halo(1)
    z_step(3)
    wait_halo(0)
    attend(0, 0, 2)
    give_back(0, 0)
    relay(1)
    attend(0, 2, 4)
    give_back(0, 1)
    z_step(4)
    y_step(0)
    wait_halo(1)
    attend(1, 0, 2)
    give_back(1, 0)
    attend(1, 2, 4)
    give_back(1, 1)
    y_step(1)
    settle(0)
    ex0 = exchange(0)
    settle(1)
    ex1 = exchange(1)
    y_step(2)
    for op in (ex2, ex0, ex1):
        op.wait_recv()
    for op in passed:
        op.wait_recv()

    def part(dest, n):
        total = None
        for side in range(2):
            if side == 0:
                rows = [fin[i, dest, core] for i in range(3)]
            else:
                rows = [par[i, dest] for i in range(3)]
            wt = wbuf[side, pl.ds(2 * n, 2)].reshape(768, 384)
            p = lax.dot_general(jnp.concatenate(rows, axis=1), wt, (((1,), (1,)), ((), ())),
                                preferred_element_type=F32)
            total = p if total is None else total + p
        return total

    up, down, far = lax.rem(x + 1, 4), lax.rem(x + 3, 4), lax.rem(x + 2, 4)
    fars = []
    for n in (0, 2, 1, 3):
        far_out[n] = part(far, n).astype(BF)
        fars.append(push(far_out.at[n], far_in.at[n], far_send.at[n], far_recv.at[n], x_up if n < 2 else x_down))
    nears = []
    for n in range(2):
        near_out[0, 2 + n] = part(up, 2 + n).astype(BF)
        nears.append(push(near_out.at[0, 2 + n], near_in.at[0, 2 + n], near_send.at[0, 2 + n],
                          near_recv.at[0, 2 + n], x_up))
        near_out[1, n] = part(down, n).astype(BF)
        nears.append(push(near_out.at[1, n], near_in.at[1, n], near_send.at[1, n],
                          near_recv.at[1, n], x_down))
    for n in range(4):
        own[n] = part(x, n)
    for n in range(2):
        fars[0 if n == 0 else 2].wait_recv()
        near_out[0, n] = (part(up, n) + far_in[n].astype(F32)).astype(BF)
        nears.append(push(near_out.at[0, n], near_in.at[0, n], near_send.at[0, n],
                          near_recv.at[0, n], x_up))
        fars[1 if n == 0 else 3].wait_recv()
        near_out[1, 2 + n] = (part(down, 2 + n) + far_in[2 + n].astype(F32)).astype(BF)
        nears.append(push(near_out.at[1, 2 + n], near_in.at[1, 2 + n], near_send.at[1, 2 + n],
                          near_recv.at[1, 2 + n], x_down))
    for op in nears:
        op.wait_recv()
    for n in range(4):
        total = own[n] + near_in[0, n].astype(F32) + near_in[1, n].astype(F32)
        out_ref[:, n * 768:(n + 1) * 768] = total.astype(BF)

    for slot in range(2):
        sent = snd.at[slot, pl.ds(0, NS - 1)]
        pltpu.make_async_copy(sent, sent, snd_sem.at[slot]).wait()
        back = ret.at[slot, pl.ds(0, NS - 1)]
        pltpu.make_async_copy(back, back, ret_send.at[slot]).wait()
    for slot in range(3):
        kv = kvs[slot]
        for side in range(2):
            out = kv.at[:, pl.ds(4, 4)]
            pltpu.make_async_copy(out, out, halo_send.at[slot, side]).wait()

            @pl.when(edge[1 - side])
            def _():
                pltpu.make_async_copy(rly.at[slot], rly.at[slot], fwd_send.at[slot]).wait()
    for op in [ex0, ex1, ex2] + ys + passed + rights + lefts + fars + nears:
        op.wait_send()


def attention(queries, keys, values, wt, head_kind, band_offsets):
    vm = pl.BlockSpec(memory_space=pltpu.VMEM)
    sm = pl.BlockSpec(memory_space=pltpu.SMEM)
    dma = pltpu.SemaphoreType.DMA
    return pl.pallas_call(
        kernel,
        out_shape=jax.ShapeDtypeStruct((128, 3072), BF),
        in_specs=[sm, sm, vm, vm, vm, vm],
        out_specs=vm,
        scratch_shapes=[
            pltpu.VMEM((2, NS, 3, 2, 16, DH), BF),
            pltpu.VMEM((2, 3, 4, 16, 16, DH), BF),
            pltpu.VMEM((3, 4, 16, 16, DH), BF),
            pltpu.VMEM((2, 12, 16, 16, DH), BF),
            pltpu.VMEM((2, 12, 16, 16, DH), BF),
            pltpu.VMEM((2, 12, 16, 16, DH), BF),
            pltpu.VMEM((3, 4, 16, 16, DH), BF),
            pltpu.VMEM((2, NS, 2, 16, DH), BF),
            pltpu.VMEM((2, 8, 4, 96, 384), BF),
            pltpu.VMEM((3, 2, 2, 16, 16, DH), BF),
            pltpu.VMEM((3, 4, 2, DH, DH), BF),
            pltpu.VMEM((3, 4, DH, DH), BF),
            pltpu.VMEM((4, DH, 768), BF),
            pltpu.VMEM((4, DH, 768), BF),
            pltpu.VMEM((2, 4, DH, 768), BF),
            pltpu.VMEM((2, 4, DH, 768), BF),
            pltpu.VMEM((4, DH, 768), F32),
            dma((2,)), dma((2,)), dma((3, 2)), dma((3, 2)), dma((3,)), dma((3,)), dma((3,)),
            dma((2,)), dma((2,)),
            dma((4,)), dma((4,)), dma((4,)), dma((4,)), dma((3,)), dma((3,)), dma((4,)), dma((4,)),
            dma((3,)), dma((3,)), dma((4,)), dma((4,)), dma((2, 4)), dma((2, 4)),
        ],
        compiler_params=pltpu.CompilerParams(
            collective_id=0, has_side_effects=True, vmem_limit_bytes=60 * 1024 * 1024),
    )(head_kind, band_offsets, queries, keys, values, wt)


def body(queries, keys, values, w_out, head_kind, band_offsets):
    return attention(queries, keys, values, w_out, head_kind, band_offsets)


def solution(mesh):
    return jax.shard_map(
        body,
        mesh=mesh,
        in_specs=(P("seq", "head"), P("seq", "head"), P("seq", "head"), P("head", "seq"), P(), P()),
        out_specs=P(("seq", "head"), None),
        check_vma=False,
    )
```

```python
import math

import jax
import jax.numpy as jnp
from jax import lax
from jax.experimental import pallas as pl
from jax.experimental.pallas import tpu as pltpu
from jax.sharding import PartitionSpec as P

DH = 128
BLK = 256
NS = 32
KOFF = 7
BF = jnp.bfloat16
F32 = jnp.float32
MESH = pl.DeviceIdType.MESH
EXP_SCALE = math.log2(math.e) / math.sqrt(DH)


def pick(cond, yes, no):
    return jnp.where(cond, yes, no)


def kernel(kind_ref, offs_ref, q_ref, k_ref, v_ref, w_ref, out_ref,
           snd, rcv, qx, kv0, kv1, kv2, att, ret, wbuf, rly, fin, par, far_out, far_in, near_out, near_in, own,
           snd_sem, rcv_sem, halo_send, halo_recv, rly_send, rly_recv, fwd_send, ret_send, ret_recv,
           wy_send, wy_recv, wr_send, wr_recv, wl_send, wl_recv, wp_send, wp_recv,
           ex_send, ex_recv, far_send, far_recv, near_send, near_recv):
    s = lax.axis_index("seq")
    g = lax.axis_index("head")
    frame = s // 2
    half = s % 2
    z = s // 4
    y = s % 4
    x = g // 2
    core = g % 2
    mate = {"head": x * 2 + 1 - core}
    x_up = {"head": lax.rem(x + 1, 4) * 2 + core}
    x_down = {"head": lax.rem(x + 3, 4) * 2 + core}
    kvs = (kv0, kv1, kv2)

    barrier = pltpu.get_barrier_semaphore()

    def greet(i, c):
        pl.semaphore_signal(barrier, inc=1, device_id={"seq": lax.rem(s + i, NS)}, device_id_type=MESH)
        return c

    lax.fori_loop(1, NS, greet, 0)
    for peer in (mate, x_up, x_down):
        pl.semaphore_signal(barrier, inc=1, device_id=peer, device_id_type=MESH)

    kinds = [kind_ref[g * 3 + i] for i in range(3)]
    sp0 = kinds[0] == 0
    sp2 = jnp.logical_and(kinds[0] != 0, kinds[1] != 0)
    sp1 = jnp.logical_and(kinds[0] != 0, kinds[1] == 0)
    kind_slot = (jnp.where(sp0, kinds[1], kinds[0]), jnp.where(sp2, kinds[1], kinds[2]), 0)

    srcs = (q_ref, k_ref, v_ref)

    def prep(r, c):
        rows = pl.ds(pl.multiple_of(r * 128, 128), 128)
        for t in range(3):
            a = srcs[t][rows, 0:128]
            b = srcs[t][rows, 128:256]
            d = srcs[t][rows, 256:384]
            x0 = pick(sp0, b, a)
            x1 = pick(sp2, b, d)
            snd[0, pl.ds(r * 4, 4), t] = x0.reshape(4, 2, 16, DH)
            snd[1, pl.ds(r * 4, 4), t] = x1.reshape(4, 2, 16, DH)
            x2 = pick(sp0, a, pick(sp2, d, b)).reshape(8, 16, DH)
            blk = r // 2
            part = pl.ds((r % 2) * 8, 8)
            if t == 0:
                qx[2, blk, part] = x2
            else:
                kv2[t - 1, 4 + blk, part] = x2
        return c

    lax.fori_loop(0, 8, prep, 0)
    wa, wb, wd = w_ref[0:DH], w_ref[DH:2 * DH], w_ref[2 * DH:]
    w_rows = jnp.concatenate(
        [pick(sp0, wb, wa), pick(sp2, wb, wd), pick(sp0, wa, pick(sp2, wd, wb))], axis=0)
    eye = (lax.broadcasted_iota(jnp.int32, (96, 96), 0)
           == lax.broadcasted_iota(jnp.int32, (96, 96), 1)).astype(F32).astype(BF)
    wbuf[0, z, y] = lax.dot_general(
        eye, w_rows, (((1,), (1,)), ((), ())), preferred_element_type=F32).astype(BF)
    pl.semaphore_wait(barrier, NS + 2)

    def scatter(slot):
        def go(i, c):
            d = lax.rem(s + i, NS)
            pltpu.make_async_remote_copy(
                src_ref=snd.at[slot, d],
                dst_ref=rcv.at[slot, :, pl.ds(half * 2, 2), frame],
                send_sem=snd_sem.at[slot], recv_sem=rcv_sem.at[slot],
                device_id={"seq": d}, device_id_type=MESH).start()
            return c
        lax.fori_loop(1, NS, go, 0)
        pltpu.make_async_copy(
            snd.at[slot, s], rcv.at[slot, :, pl.ds(half * 2, 2), frame], rcv_sem.at[slot]).start()

    edge = (y == 3, y == 0)
    hop = (1, NS - 1)
    lows = (0, 8)

    def halo(slot):
        kv = kvs[slot]
        for side in range(2):
            lo = lows[side]
            peer = lax.rem(s + hop[side], NS)
            pltpu.make_async_remote_copy(
                src_ref=kv.at[:, pl.ds(4, 2)], dst_ref=kv.at[:, pl.ds(lo, 2)],
                send_sem=halo_send.at[slot, side], recv_sem=halo_recv.at[slot, side],
                device_id={"seq": peer}, device_id_type=MESH).start()

            @pl.when(jnp.logical_not(edge[side]))
            def _():
                pltpu.make_async_remote_copy(
                    src_ref=kv.at[:, pl.ds(6, 2)], dst_ref=kv.at[:, pl.ds(lo + 2, 2)],
                    send_sem=halo_send.at[slot, side], recv_sem=halo_recv.at[slot, side],
                    device_id={"seq": peer}, device_id_type=MESH).start()

            @pl.when(edge[side])
            def _():
                pltpu.make_async_remote_copy(
                    src_ref=kv.at[:, pl.ds(6, 2)], dst_ref=rly.at[slot],
                    send_sem=halo_send.at[slot, side], recv_sem=rly_recv.at[slot],
                    device_id={"seq": z * 4 + (0 if side == 0 else 3)}, device_id_type=MESH).start()

    def relay(slot):
        kv = kvs[slot]
        for side in range(2):
            lo = lows[side]

            @pl.when(edge[1 - side])
            def _():
                pltpu.make_async_copy(rly.at[slot], rly.at[slot], rly_recv.at[slot]).wait()
                pltpu.make_async_remote_copy(
                    src_ref=rly.at[slot], dst_ref=kv.at[:, pl.ds(lo + 2, 2)],
                    send_sem=fwd_send.at[slot], recv_sem=halo_recv.at[slot, side],
                    device_id={"seq": lax.rem(z + (1 if side == 0 else 7), 8) * 4 + y},
                    device_id_type=MESH).start()

    def wait_halo(slot):
        kv = kvs[slot]
        for side in range(2):
            got = kv.at[:, pl.ds(lows[side], 4)]
            pltpu.make_async_copy(got, got, halo_recv.at[slot, side]).wait()

    def attend(slot, first=0, last=4):
        kv = kvs[slot]
        offs = [jnp.where(kind_slot[slot] == 1, offs_ref[1, o], offs_ref[0, o]) for o in range(KOFF)]
        ones = jnp.ones((BLK, DH), BF)

        def block(j, c):
            q = qx[slot, j].reshape(BLK, DH)
            ks, vs, pens = [], [], []
            for o in range(KOFF):
                t = j + offs[o]
                gb = s * 4 + t
                ok = jnp.logical_and(gb >= 0, gb < NS * 4)
                idx = jnp.where(ok, t + 4, j + 4)
                ks.append(kv[0, idx].reshape(BLK, DH))
                vs.append(jnp.concatenate([kv[1, idx].reshape(BLK, DH), ones], axis=1))
                pens.append(jnp.where(ok, 0.0, 1e30).astype(F32))
            sc = [lax.dot_general(q, k, (((1,), (1,)), ((), ())), preferred_element_type=F32) for k in ks]
            m = sc[0]
            for x in sc[1:]:
                m = jnp.maximum(m, x)
            mx = jnp.max(m, axis=1, keepdims=True) * EXP_SCALE
            ps = [jnp.exp2(x * EXP_SCALE - (mx + pen)).astype(BF) for x, pen in zip(sc, pens)]
            acc = jnp.dot(jnp.concatenate(ps, axis=1), jnp.concatenate(vs, axis=0),
                          preferred_element_type=F32)
            o = (acc[:, :DH] / acc[:, DH:]).astype(BF)
            att[slot, j] = o.reshape(16, 16, DH)
            return c

        lax.fori_loop(first, last, block, 0)

    def wait_slot(slot):
        pltpu.make_async_copy(rcv.at[slot], rcv.at[slot], rcv_sem.at[slot]).wait()

    def choose(slot):
        temporal = kind_slot[slot] == 1

        def sel(b, c):
            for t in range(3):
                local = snd[slot, pl.ds(b * 8, 8), t].reshape(16, 16, DH)
                x = pick(temporal, rcv[slot, t, b], local)
                if t == 0:
                    qx[slot, b] = x
                else:
                    kvs[slot][t - 1, 4 + b] = x
            return c

        lax.fori_loop(0, 4, sel, 0)

    def give_back(slot, side):
        def go(i, c):
            to = lax.rem(frame + i, 16)
            pltpu.make_async_remote_copy(
                src_ref=att.at[slot, side * 2:side * 2 + 2, to],
                dst_ref=ret.at[slot, s],
                send_sem=ret_send.at[slot], recv_sem=ret_recv.at[slot],
                device_id={"seq": to * 2 + side}, device_id_type=MESH).start()
            return c
        lax.fori_loop(1, 16, go, 0)

        @pl.when(half == side)
        def _():
            pltpu.make_async_copy(
                att.at[slot, side * 2:side * 2 + 2, frame], ret.at[slot, s], ret_recv.at[slot]).start()

        @pl.when(half != side)
        def _():
            pltpu.make_async_remote_copy(
                src_ref=att.at[slot, side * 2:side * 2 + 2, frame],
                dst_ref=ret.at[slot, s],
                send_sem=ret_send.at[slot], recv_sem=ret_recv.at[slot],
                device_id={"seq": frame * 2 + side}, device_id_type=MESH).start()

    def push(src_ref, dst_ref, send, recv, peer):
        op = pltpu.make_async_remote_copy(
            src_ref=src_ref, dst_ref=dst_ref, send_sem=send, recv_sem=recv,
            device_id=peer, device_id_type=MESH)
        op.start()
        return op

    y_up = {"seq": z * 4 + lax.rem(y + 1, 4)}
    y_down = {"seq": z * 4 + lax.rem(y + 3, 4)}
    z_up = {"seq": lax.rem(z + 1, 8) * 4 + y}
    z_down = {"seq": lax.rem(z + 7, 8) * 4 + y}

    def w_right(t):
        row = wbuf.at[0, lax.rem(z + 8 - t, 8), y]
        return push(row, row, wr_send.at[t], wr_recv.at[t], z_up)

    def w_left(t):
        row = wbuf.at[0, lax.rem(z + t, 8), y]
        return push(row, row, wl_send.at[t], wl_recv.at[t], z_down)

    def exchange(slot):
        return push(fin.at[slot, :, 1 - core], par.at[slot], ex_send.at[slot], ex_recv.at[slot], mate)

    def settle(slot):
        pltpu.make_async_copy(ret.at[slot], ret.at[slot], ret_recv.at[slot]).wait()
        temporal = kind_slot[slot] == 1

        def go(t, c):
            got = ret[slot, pl.ds(t * 4, 4)].reshape(DH, DH)
            mine = att[slot, t // 2, pl.ds((t % 2) * 8, 8)].reshape(DH, DH)
            fin[slot, t // 2, t % 2] = pick(temporal, got, mine)
            return c

        lax.fori_loop(0, 8, go, 0)

    passed = []
    columns = (y, lax.rem(y + 3, 4), lax.rem(y + 1, 4), lax.rem(y + 2, 4))

    def pass_column(i):
        passed.append(push(wbuf.at[0, :, columns[i]], wbuf.at[1, :, columns[i]],
                           wp_send.at[i], wp_recv.at[i], mate))

    def z_step(t):
        if t > 0:
            rights[t - 1].wait_recv()
            if t <= 3:
                lefts[t - 1].wait_recv()
        if t < 4:
            rights.append(w_right(t))
        if t < 3:
            lefts.append(w_left(t))

    def y_step(t):
        if t == 0:
            part = wbuf.at[0, :, y]
            ys.append(push(part, part, wy_send.at[0], wy_recv.at[0], y_up))
            ys.append(push(part, part, wy_send.at[1], wy_recv.at[1], y_down))
            pass_column(0)
        elif t == 1:
            ys[0].wait_recv()
            part = wbuf.at[0, pl.ds(0, 4), columns[1]]
            ys.append(push(part, part, wy_send.at[2], wy_recv.at[2], y_up))
            ys[1].wait_recv()
            part = wbuf.at[0, pl.ds(4, 4), columns[2]]
            ys.append(push(part, part, wy_send.at[3], wy_recv.at[3], y_down))
            pass_column(1)
            pass_column(2)
        else:
            ys[2].wait_recv()
            ys[3].wait_recv()
            pass_column(3)

    rights, lefts, ys = [], [], []
    scatter(0)
    z_step(0)
    halo(2)
    relay(2)
    wait_slot(0)
    scatter(1)
    z_step(1)
    choose(0)
    halo(0)
    z_step(2)
    wait_halo(2)
    attend(2)

    def spatial(t, c):
        fin[2, t // 2, t % 2] = att[2, t // 2, pl.ds((t % 2) * 8, 8)].reshape(DH, DH)
        return c

    lax.fori_loop(0, 8, spatial, 0)
    ex2 = exchange(2)
    z_step(3)
    relay(0)
    wait_slot(1)
    choose(1)
    halo(1)
    z_step(4)
    y_step(0)
    wait_halo(0)
    attend(0, 0, 2)
    give_back(0, 0)
    relay(1)
    attend(0, 2, 4)
    give_back(0, 1)
    wait_halo(1)
    attend(1, 0, 2)
    give_back(1, 0)
    attend(1, 2, 4)
    give_back(1, 1)
    y_step(1)
    settle(0)
    ex0 = exchange(0)
    settle(1)
    ex1 = exchange(1)
    y_step(2)
    for op in (ex2, ex0, ex1):
        op.wait_recv()
    for op in passed:
        op.wait_recv()

    def part(dest, n):
        total = None
        for side in range(2):
            if side == 0:
                rows = [fin[i, dest, core] for i in range(3)]
            else:
                rows = [par[i, dest] for i in range(3)]
            wt = wbuf[side, pl.ds(2 * n, 2)].reshape(768, 384)
            p = lax.dot_general(jnp.concatenate(rows, axis=1), wt, (((1,), (1,)), ((), ())),
                                preferred_element_type=F32)
            total = p if total is None else total + p
        return total

    up, down, far = lax.rem(x + 1, 4), lax.rem(x + 3, 4), lax.rem(x + 2, 4)
    fars = []
    for n in (0, 2, 1, 3):
        far_out[n] = part(far, n).astype(BF)
        fars.append(push(far_out.at[n], far_in.at[n], far_send.at[n], far_recv.at[n], x_up if n < 2 else x_down))
    nears = []
    for n in range(2):
        near_out[0, 2 + n] = part(up, 2 + n).astype(BF)
        nears.append(push(near_out.at[0, 2 + n], near_in.at[0, 2 + n], near_send.at[0, 2 + n],
                          near_recv.at[0, 2 + n], x_up))
        near_out[1, n] = part(down, n).astype(BF)
        nears.append(push(near_out.at[1, n], near_in.at[1, n], near_send.at[1, n],
                          near_recv.at[1, n], x_down))
    for n in range(4):
        own[n] = part(x, n)
    for n in range(2):
        fars[0 if n == 0 else 2].wait_recv()
        near_out[0, n] = (part(up, n) + far_in[n].astype(F32)).astype(BF)
        nears.append(push(near_out.at[0, n], near_in.at[0, n], near_send.at[0, n],
                          near_recv.at[0, n], x_up))
        fars[1 if n == 0 else 3].wait_recv()
        near_out[1, 2 + n] = (part(down, 2 + n) + far_in[2 + n].astype(F32)).astype(BF)
        nears.append(push(near_out.at[1, 2 + n], near_in.at[1, 2 + n], near_send.at[1, 2 + n],
                          near_recv.at[1, 2 + n], x_down))
    for op in nears:
        op.wait_recv()
    for n in range(4):
        total = own[n] + near_in[0, n].astype(F32) + near_in[1, n].astype(F32)
        out_ref[:, n * 768:(n + 1) * 768] = total.astype(BF)

    for slot in range(2):
        sent = snd.at[slot, pl.ds(0, NS - 1)]
        pltpu.make_async_copy(sent, sent, snd_sem.at[slot]).wait()
        back = ret.at[slot, pl.ds(0, NS - 1)]
        pltpu.make_async_copy(back, back, ret_send.at[slot]).wait()
    for slot in range(3):
        kv = kvs[slot]
        for side in range(2):
            out = kv.at[:, pl.ds(4, 4)]
            pltpu.make_async_copy(out, out, halo_send.at[slot, side]).wait()

            @pl.when(edge[1 - side])
            def _():
                pltpu.make_async_copy(rly.at[slot], rly.at[slot], fwd_send.at[slot]).wait()
    for op in [ex0, ex1, ex2] + ys + passed + rights + lefts + fars + nears:
        op.wait_send()


def attention(queries, keys, values, wt, head_kind, band_offsets):
    vm = pl.BlockSpec(memory_space=pltpu.VMEM)
    sm = pl.BlockSpec(memory_space=pltpu.SMEM)
    dma = pltpu.SemaphoreType.DMA
    return pl.pallas_call(
        kernel,
        out_shape=jax.ShapeDtypeStruct((128, 3072), BF),
        in_specs=[sm, sm, vm, vm, vm, vm],
        out_specs=vm,
        scratch_shapes=[
            pltpu.VMEM((2, NS, 3, 2, 16, DH), BF),
            pltpu.VMEM((2, 3, 4, 16, 16, DH), BF),
            pltpu.VMEM((3, 4, 16, 16, DH), BF),
            pltpu.VMEM((2, 12, 16, 16, DH), BF),
            pltpu.VMEM((2, 12, 16, 16, DH), BF),
            pltpu.VMEM((2, 12, 16, 16, DH), BF),
            pltpu.VMEM((3, 4, 16, 16, DH), BF),
            pltpu.VMEM((2, NS, 2, 16, DH), BF),
            pltpu.VMEM((2, 8, 4, 96, 384), BF),
            pltpu.VMEM((3, 2, 2, 16, 16, DH), BF),
            pltpu.VMEM((3, 4, 2, DH, DH), BF),
            pltpu.VMEM((3, 4, DH, DH), BF),
            pltpu.VMEM((4, DH, 768), BF),
            pltpu.VMEM((4, DH, 768), BF),
            pltpu.VMEM((2, 4, DH, 768), BF),
            pltpu.VMEM((2, 4, DH, 768), BF),
            pltpu.VMEM((4, DH, 768), F32),
            dma((2,)), dma((2,)), dma((3, 2)), dma((3, 2)), dma((3,)), dma((3,)), dma((3,)),
            dma((2,)), dma((2,)),
            dma((4,)), dma((4,)), dma((4,)), dma((4,)), dma((3,)), dma((3,)), dma((4,)), dma((4,)),
            dma((3,)), dma((3,)), dma((4,)), dma((4,)), dma((2, 4)), dma((2, 4)),
        ],
        compiler_params=pltpu.CompilerParams(
            collective_id=0, has_side_effects=True, vmem_limit_bytes=60 * 1024 * 1024),
    )(head_kind, band_offsets, queries, keys, values, wt)


def body(queries, keys, values, w_out, head_kind, band_offsets):
    return attention(queries, keys, values, w_out, head_kind, band_offsets)


def solution(mesh):
    return jax.shard_map(
        body,
        mesh=mesh,
        in_specs=(P("seq", "head"), P("seq", "head"), P("seq", "head"), P("head", "seq"), P(), P()),
        out_specs=P(("seq", "head"), None),
        check_vma=False,
    )
```

```python
import math

import jax
import jax.numpy as jnp
from jax import lax
from jax.experimental import pallas as pl
from jax.experimental.pallas import tpu as pltpu
from jax.sharding import PartitionSpec as P

DH = 128
BLK = 256
NS = 32
KOFF = 7
BF = jnp.bfloat16
F32 = jnp.float32
MESH = pl.DeviceIdType.MESH
EXP_SCALE = math.log2(math.e) / math.sqrt(DH)


def pick(cond, yes, no):
    return jnp.where(cond, yes, no)


def kernel(kind_ref, offs_ref, q_ref, k_ref, v_ref, w_ref, out_ref,
           snd, rcv, qx, kv0, kv1, kv2, att, ret, wbuf, rly, fin, par, far_out, far_in, near_out, near_in, own,
           snd_sem, rcv_sem, halo_send, halo_recv, rly_send, rly_recv, fwd_send, ret_send, ret_recv,
           wy_send, wy_recv, wr_send, wr_recv, wl_send, wl_recv, wp_send, wp_recv,
           ex_send, ex_recv, far_send, far_recv, near_send, near_recv):
    s = lax.axis_index("seq")
    g = lax.axis_index("head")
    frame = s // 2
    half = s % 2
    z = s // 4
    y = s % 4
    x = g // 2
    core = g % 2
    mate = {"head": x * 2 + 1 - core}
    x_up = {"head": lax.rem(x + 1, 4) * 2 + core}
    x_down = {"head": lax.rem(x + 3, 4) * 2 + core}
    kvs = (kv0, kv1, kv2)

    barrier = pltpu.get_barrier_semaphore()

    def greet(i, c):
        pl.semaphore_signal(barrier, inc=1, device_id={"seq": lax.rem(s + i, NS)}, device_id_type=MESH)
        return c

    lax.fori_loop(1, NS, greet, 0)
    for peer in (mate, x_up, x_down):
        pl.semaphore_signal(barrier, inc=1, device_id=peer, device_id_type=MESH)

    kinds = [kind_ref[g * 3 + i] for i in range(3)]
    sp0 = kinds[0] == 0
    sp2 = jnp.logical_and(kinds[0] != 0, kinds[1] != 0)
    sp1 = jnp.logical_and(kinds[0] != 0, kinds[1] == 0)
    kind_slot = (jnp.where(sp0, kinds[1], kinds[0]), jnp.where(sp2, kinds[1], kinds[2]), 0)

    srcs = (q_ref, k_ref, v_ref)

    def prep(r, c):
        rows = pl.ds(pl.multiple_of(r * 128, 128), 128)
        for t in range(3):
            a = srcs[t][rows, 0:128]
            b = srcs[t][rows, 128:256]
            d = srcs[t][rows, 256:384]
            x0 = pick(sp0, b, a)
            x1 = pick(sp2, b, d)
            snd[0, pl.ds(r * 4, 4), t] = x0.reshape(4, 2, 16, DH)
            snd[1, pl.ds(r * 4, 4), t] = x1.reshape(4, 2, 16, DH)
            x2 = pick(sp0, a, pick(sp2, d, b)).reshape(8, 16, DH)
            blk = r // 2
            part = pl.ds((r % 2) * 8, 8)
            if t == 0:
                qx[2, blk, part] = x2
            else:
                kv2[t - 1, 4 + blk, part] = x2
        return c

    lax.fori_loop(0, 8, prep, 0)
    wa, wb, wd = w_ref[0:DH], w_ref[DH:2 * DH], w_ref[2 * DH:]
    w_rows = jnp.concatenate(
        [pick(sp0, wb, wa), pick(sp2, wb, wd), pick(sp0, wa, pick(sp2, wd, wb))], axis=0)
    eye = (lax.broadcasted_iota(jnp.int32, (96, 96), 0)
           == lax.broadcasted_iota(jnp.int32, (96, 96), 1)).astype(F32).astype(BF)
    wbuf[0, z, y] = lax.dot_general(
        eye, w_rows, (((1,), (1,)), ((), ())), preferred_element_type=F32).astype(BF)
    pl.semaphore_wait(barrier, NS + 2)

    def scatter(slot):
        def go(i, c):
            d = lax.rem(s + i, NS)
            pltpu.make_async_remote_copy(
                src_ref=snd.at[slot, d],
                dst_ref=rcv.at[slot, :, pl.ds(half * 2, 2), frame],
                send_sem=snd_sem.at[slot], recv_sem=rcv_sem.at[slot],
                device_id={"seq": d}, device_id_type=MESH).start()
            return c
        lax.fori_loop(1, NS, go, 0)
        pltpu.make_async_copy(
            snd.at[slot, s], rcv.at[slot, :, pl.ds(half * 2, 2), frame], rcv_sem.at[slot]).start()

    edge = (y == 3, y == 0)
    hop = (1, NS - 1)
    lows = (0, 8)

    def halo(slot):
        kv = kvs[slot]
        for side in range(2):
            lo = lows[side]
            peer = lax.rem(s + hop[side], NS)
            pltpu.make_async_remote_copy(
                src_ref=kv.at[:, pl.ds(4, 2)], dst_ref=kv.at[:, pl.ds(lo, 2)],
                send_sem=halo_send.at[slot, side], recv_sem=halo_recv.at[slot, side],
                device_id={"seq": peer}, device_id_type=MESH).start()

            @pl.when(jnp.logical_not(edge[side]))
            def _():
                pltpu.make_async_remote_copy(
                    src_ref=kv.at[:, pl.ds(6, 2)], dst_ref=kv.at[:, pl.ds(lo + 2, 2)],
                    send_sem=halo_send.at[slot, side], recv_sem=halo_recv.at[slot, side],
                    device_id={"seq": peer}, device_id_type=MESH).start()

            @pl.when(edge[side])
            def _():
                pltpu.make_async_remote_copy(
                    src_ref=kv.at[:, pl.ds(6, 2)], dst_ref=rly.at[slot],
                    send_sem=halo_send.at[slot, side], recv_sem=rly_recv.at[slot],
                    device_id={"seq": z * 4 + (0 if side == 0 else 3)}, device_id_type=MESH).start()

    def relay(slot):
        kv = kvs[slot]
        for side in range(2):
            lo = lows[side]

            @pl.when(edge[1 - side])
            def _():
                pltpu.make_async_copy(rly.at[slot], rly.at[slot], rly_recv.at[slot]).wait()
                pltpu.make_async_remote_copy(
                    src_ref=rly.at[slot], dst_ref=kv.at[:, pl.ds(lo + 2, 2)],
                    send_sem=fwd_send.at[slot], recv_sem=halo_recv.at[slot, side],
                    device_id={"seq": lax.rem(z + (1 if side == 0 else 7), 8) * 4 + y},
                    device_id_type=MESH).start()

    def wait_halo(slot):
        kv = kvs[slot]
        for side in range(2):
            got = kv.at[:, pl.ds(lows[side], 4)]
            pltpu.make_async_copy(got, got, halo_recv.at[slot, side]).wait()

    def attend(slot, first=0, last=4):
        kv = kvs[slot]
        offs = [jnp.where(kind_slot[slot] == 1, offs_ref[1, o], offs_ref[0, o]) for o in range(KOFF)]
        ones = jnp.ones((BLK, DH), BF)

        def block(j, c):
            q = qx[slot, j].reshape(BLK, DH)
            ks, vs, pens = [], [], []
            for o in range(KOFF):
                t = j + offs[o]
                gb = s * 4 + t
                ok = jnp.logical_and(gb >= 0, gb < NS * 4)
                idx = jnp.where(ok, t + 4, j + 4)
                ks.append(kv[0, idx].reshape(BLK, DH))
                vs.append(jnp.concatenate([kv[1, idx].reshape(BLK, DH), ones], axis=1))
                pens.append(jnp.where(ok, 0.0, 1e30).astype(F32))
            sc = [lax.dot_general(q, k, (((1,), (1,)), ((), ())), preferred_element_type=F32) for k in ks]
            m = sc[0]
            for x in sc[1:]:
                m = jnp.maximum(m, x)
            mx = jnp.max(m, axis=1, keepdims=True) * EXP_SCALE
            ps = [jnp.exp2(x * EXP_SCALE - (mx + pen)).astype(BF) for x, pen in zip(sc, pens)]
            acc = jnp.dot(jnp.concatenate(ps, axis=1), jnp.concatenate(vs, axis=0),
                          preferred_element_type=F32)
            o = (acc[:, :DH] / acc[:, DH:]).astype(BF)
            att[slot, j] = o.reshape(16, 16, DH)
            return c

        lax.fori_loop(first, last, block, 0)

    def wait_slot(slot):
        pltpu.make_async_copy(rcv.at[slot], rcv.at[slot], rcv_sem.at[slot]).wait()

    def choose(slot):
        temporal = kind_slot[slot] == 1

        def sel(b, c):
            for t in range(3):
                local = snd[slot, pl.ds(b * 8, 8), t].reshape(16, 16, DH)
                x = pick(temporal, rcv[slot, t, b], local)
                if t == 0:
                    qx[slot, b] = x
                else:
                    kvs[slot][t - 1, 4 + b] = x
            return c

        lax.fori_loop(0, 4, sel, 0)

    def give_back(slot, side):
        def go(i, c):
            to = lax.rem(frame + i, 16)
            pltpu.make_async_remote_copy(
                src_ref=att.at[slot, side * 2:side * 2 + 2, to],
                dst_ref=ret.at[slot, s],
                send_sem=ret_send.at[slot], recv_sem=ret_recv.at[slot],
                device_id={"seq": to * 2 + side}, device_id_type=MESH).start()
            return c
        lax.fori_loop(1, 16, go, 0)

        @pl.when(half == side)
        def _():
            pltpu.make_async_copy(
                att.at[slot, side * 2:side * 2 + 2, frame], ret.at[slot, s], ret_recv.at[slot]).start()

        @pl.when(half != side)
        def _():
            pltpu.make_async_remote_copy(
                src_ref=att.at[slot, side * 2:side * 2 + 2, frame],
                dst_ref=ret.at[slot, s],
                send_sem=ret_send.at[slot], recv_sem=ret_recv.at[slot],
                device_id={"seq": frame * 2 + side}, device_id_type=MESH).start()

    def push(src_ref, dst_ref, send, recv, peer):
        op = pltpu.make_async_remote_copy(
            src_ref=src_ref, dst_ref=dst_ref, send_sem=send, recv_sem=recv,
            device_id=peer, device_id_type=MESH)
        op.start()
        return op

    y_up = {"seq": z * 4 + lax.rem(y + 1, 4)}
    y_down = {"seq": z * 4 + lax.rem(y + 3, 4)}
    z_up = {"seq": lax.rem(z + 1, 8) * 4 + y}
    z_down = {"seq": lax.rem(z + 7, 8) * 4 + y}

    def w_right(t):
        row = wbuf.at[0, lax.rem(z + 8 - t, 8), y]
        return push(row, row, wr_send.at[t], wr_recv.at[t], z_up)

    def w_left(t):
        row = wbuf.at[0, lax.rem(z + t, 8), y]
        return push(row, row, wl_send.at[t], wl_recv.at[t], z_down)

    def exchange(slot):
        return push(fin.at[slot, :, 1 - core], par.at[slot], ex_send.at[slot], ex_recv.at[slot], mate)

    def settle(slot):
        pltpu.make_async_copy(ret.at[slot], ret.at[slot], ret_recv.at[slot]).wait()
        temporal = kind_slot[slot] == 1

        def go(t, c):
            got = ret[slot, pl.ds(t * 4, 4)].reshape(DH, DH)
            mine = att[slot, t // 2, pl.ds((t % 2) * 8, 8)].reshape(DH, DH)
            fin[slot, t // 2, t % 2] = pick(temporal, got, mine)
            return c

        lax.fori_loop(0, 8, go, 0)

    passed = []
    columns = (y, lax.rem(y + 3, 4), lax.rem(y + 1, 4), lax.rem(y + 2, 4))

    def pass_column(i):
        passed.append(push(wbuf.at[0, :, columns[i]], wbuf.at[1, :, columns[i]],
                           wp_send.at[i], wp_recv.at[i], mate))

    def z_step(t):
        if t > 0:
            rights[t - 1].wait_recv()
            if t <= 3:
                lefts[t - 1].wait_recv()
        if t < 4:
            rights.append(w_right(t))
        if t < 3:
            lefts.append(w_left(t))

    def y_step(t):
        if t == 0:
            part = wbuf.at[0, :, y]
            ys.append(push(part, part, wy_send.at[0], wy_recv.at[0], y_up))
            ys.append(push(part, part, wy_send.at[1], wy_recv.at[1], y_down))
            pass_column(0)
        elif t == 1:
            ys[0].wait_recv()
            part = wbuf.at[0, pl.ds(0, 4), columns[1]]
            ys.append(push(part, part, wy_send.at[2], wy_recv.at[2], y_up))
            ys[1].wait_recv()
            part = wbuf.at[0, pl.ds(4, 4), columns[2]]
            ys.append(push(part, part, wy_send.at[3], wy_recv.at[3], y_down))
            pass_column(1)
            pass_column(2)
        else:
            ys[2].wait_recv()
            ys[3].wait_recv()
            pass_column(3)

    rights, lefts, ys = [], [], []
    scatter(0)
    z_step(0)
    halo(2)
    relay(2)
    wait_slot(0)
    scatter(1)
    z_step(1)
    choose(0)
    halo(0)
    z_step(2)
    wait_halo(2)
    attend(2)

    def spatial(t, c):
        fin[2, t // 2, t % 2] = att[2, t // 2, pl.ds((t % 2) * 8, 8)].reshape(DH, DH)
        return c

    lax.fori_loop(0, 8, spatial, 0)
    ex2 = exchange(2)
    z_step(3)
    relay(0)
    wait_slot(1)
    choose(1)
    halo(1)
    z_step(4)
    y_step(0)
    wait_halo(0)
    attend(0, 0, 2)
    give_back(0, 0)
    relay(1)
    attend(0, 2, 4)
    give_back(0, 1)
    wait_halo(1)
    attend(1, 0, 2)
    give_back(1, 0)
    y_step(1)
    attend(1, 2, 4)
    give_back(1, 1)
    settle(0)
    ex0 = exchange(0)
    settle(1)
    ex1 = exchange(1)
    y_step(2)
    for op in (ex2, ex0, ex1):
        op.wait_recv()
    for op in passed:
        op.wait_recv()

    def part(dest, n):
        total = None
        for side in range(2):
            if side == 0:
                rows = [fin[i, dest, core] for i in range(3)]
            else:
                rows = [par[i, dest] for i in range(3)]
            wt = wbuf[side, pl.ds(2 * n, 2)].reshape(768, 384)
            p = lax.dot_general(jnp.concatenate(rows, axis=1), wt, (((1,), (1,)), ((), ())),
                                preferred_element_type=F32)
            total = p if total is None else total + p
        return total

    up, down, far = lax.rem(x + 1, 4), lax.rem(x + 3, 4), lax.rem(x + 2, 4)
    fars = []
    for n in (0, 2, 1, 3):
        far_out[n] = part(far, n).astype(BF)
        fars.append(push(far_out.at[n], far_in.at[n], far_send.at[n], far_recv.at[n], x_up if n < 2 else x_down))
    nears = []
    for n in range(2):
        near_out[0, 2 + n] = part(up, 2 + n).astype(BF)
        nears.append(push(near_out.at[0, 2 + n], near_in.at[0, 2 + n], near_send.at[0, 2 + n],
                          near_recv.at[0, 2 + n], x_up))
        near_out[1, n] = part(down, n).astype(BF)
        nears.append(push(near_out.at[1, n], near_in.at[1, n], near_send.at[1, n],
                          near_recv.at[1, n], x_down))
    for n in range(4):
        own[n] = part(x, n)
    for n in range(2):
        fars[0 if n == 0 else 2].wait_recv()
        near_out[0, n] = (part(up, n) + far_in[n].astype(F32)).astype(BF)
        nears.append(push(near_out.at[0, n], near_in.at[0, n], near_send.at[0, n],
                          near_recv.at[0, n], x_up))
        fars[1 if n == 0 else 3].wait_recv()
        near_out[1, 2 + n] = (part(down, 2 + n) + far_in[2 + n].astype(F32)).astype(BF)
        nears.append(push(near_out.at[1, 2 + n], near_in.at[1, 2 + n], near_send.at[1, 2 + n],
                          near_recv.at[1, 2 + n], x_down))
    for op in nears:
        op.wait_recv()
    for n in range(4):
        total = own[n] + near_in[0, n].astype(F32) + near_in[1, n].astype(F32)
        out_ref[:, n * 768:(n + 1) * 768] = total.astype(BF)

    for slot in range(2):
        sent = snd.at[slot, pl.ds(0, NS - 1)]
        pltpu.make_async_copy(sent, sent, snd_sem.at[slot]).wait()
        back = ret.at[slot, pl.ds(0, NS - 1)]
        pltpu.make_async_copy(back, back, ret_send.at[slot]).wait()
    for slot in range(3):
        kv = kvs[slot]
        for side in range(2):
            out = kv.at[:, pl.ds(4, 4)]
            pltpu.make_async_copy(out, out, halo_send.at[slot, side]).wait()

            @pl.when(edge[1 - side])
            def _():
                pltpu.make_async_copy(rly.at[slot], rly.at[slot], fwd_send.at[slot]).wait()
    for op in [ex0, ex1, ex2] + ys + passed + rights + lefts + fars + nears:
        op.wait_send()


def attention(queries, keys, values, wt, head_kind, band_offsets):
    vm = pl.BlockSpec(memory_space=pltpu.VMEM)
    sm = pl.BlockSpec(memory_space=pltpu.SMEM)
    dma = pltpu.SemaphoreType.DMA
    return pl.pallas_call(
        kernel,
        out_shape=jax.ShapeDtypeStruct((128, 3072), BF),
        in_specs=[sm, sm, vm, vm, vm, vm],
        out_specs=vm,
        scratch_shapes=[
            pltpu.VMEM((2, NS, 3, 2, 16, DH), BF),
            pltpu.VMEM((2, 3, 4, 16, 16, DH), BF),
            pltpu.VMEM((3, 4, 16, 16, DH), BF),
            pltpu.VMEM((2, 12, 16, 16, DH), BF),
            pltpu.VMEM((2, 12, 16, 16, DH), BF),
            pltpu.VMEM((2, 12, 16, 16, DH), BF),
            pltpu.VMEM((3, 4, 16, 16, DH), BF),
            pltpu.VMEM((2, NS, 2, 16, DH), BF),
            pltpu.VMEM((2, 8, 4, 96, 384), BF),
            pltpu.VMEM((3, 2, 2, 16, 16, DH), BF),
            pltpu.VMEM((3, 4, 2, DH, DH), BF),
            pltpu.VMEM((3, 4, DH, DH), BF),
            pltpu.VMEM((4, DH, 768), BF),
            pltpu.VMEM((4, DH, 768), BF),
            pltpu.VMEM((2, 4, DH, 768), BF),
            pltpu.VMEM((2, 4, DH, 768), BF),
            pltpu.VMEM((4, DH, 768), F32),
            dma((2,)), dma((2,)), dma((3, 2)), dma((3, 2)), dma((3,)), dma((3,)), dma((3,)),
            dma((2,)), dma((2,)),
            dma((4,)), dma((4,)), dma((4,)), dma((4,)), dma((3,)), dma((3,)), dma((4,)), dma((4,)),
            dma((3,)), dma((3,)), dma((4,)), dma((4,)), dma((2, 4)), dma((2, 4)),
        ],
        compiler_params=pltpu.CompilerParams(
            collective_id=0, has_side_effects=True, vmem_limit_bytes=60 * 1024 * 1024),
    )(head_kind, band_offsets, queries, keys, values, wt)


def body(queries, keys, values, w_out, head_kind, band_offsets):
    return attention(queries, keys, values, w_out, head_kind, band_offsets)


def solution(mesh):
    return jax.shard_map(
        body,
        mesh=mesh,
        in_specs=(P("seq", "head"), P("seq", "head"), P("seq", "head"), P("head", "seq"), P(), P()),
        out_specs=P(("seq", "head"), None),
        check_vma=False,
    )
```
